32 devices in a mesh: groups: 2 (over y), docs: 4 (over z), cent: 2 (over x), sub: 2 (over core).
Axes of the slice: x: 2, y: 2, z: 4, core: 2. Of those that a mesh axis runs over, the one named last changes fastest.
Arguments:
- queries: float32 [256, 128], P(('groups', 'cent', 'sub')), parts along dimension 0, may hold values from -0.6 to 0.6
- token_codes: int32 [4, 256, 8192], P(('cent', 'sub'), ('groups', 'docs')), parts along dimension 1, may hold values from 0 to 255
- centroid_ids: int32 [4, 32768], P(('cent', 'sub'), ('groups', 'docs')), parts along dimension 1, may hold values from 0 to 4095
- slot_counts: int32 [4, 256], P(('cent', 'sub'), ('groups', 'docs')), parts along dimension 1, may hold values from 0 to 128, as said below
- centroids: bfloat16 [16384, 128], P(('cent', 'sub')), may hold values from -3 to 3
- bucket_values: float32 [16, 128], replicated, may hold values from -1.5 to 1.5
- candidates: int32 [8, 64], P(('groups', 'docs')), parts along dimension 0, may hold values from 0 to 127, as said below
- input_proj: float32 [32, 256], replicated, may hold values from -1 to 1
- gain_one: float32 [256], replicated, may hold values from 0.5 to 1.5
- query_proj: bfloat16 [256, 256], replicated, may hold values from -32 to 32, as said below
- key_proj: bfloat16 [256, 256], replicated, may hold values from -1 to 1, as said below
- value_proj: bfloat16 [256, 256], replicated, may hold values from -0.375 to 0.375
- output_proj: bfloat16 [256, 256], replicated, may hold values from -0.375 to 0.375
- gain_two: float32 [256], replicated, may hold values from 0.5 to 1.5
- up_proj: bfloat16 [256, 1024], replicated, may hold values from -0.375 to 0.375
- down_proj: bfloat16 [1024, 256], replicated, may hold values from -0.1875 to 0.1875
Outputs:
- set_states: float32 [8, 64, 256], P(('groups', 'docs'), ('cent', 'sub')), parts along dimension 0
The draws below stay inside these ranges and needn't reach their ends.
There are 2 independent parts, one for each index of `groups`. The reference program is written for one: setup_inputs(seed, part) draws one part's arguments, and reference() takes and returns one part's arrays. A program takes and returns all parts, laid end to end along the dimension named above; an argument that names none is the same for every part. Nothing has to cross between parts.
Inputs may be any that keep to these rules, and one draw needn't show every extreme that they name: `slot_counts`: for every document the counts over the 4 members sum to 256; some member holds 128 live slots of every document. The candidates of one query are distinct. `query_proj`: entries lie within the bounds below. `key_proj`: entries lie within the bounds below.
All inputs are finite; a program needn't handle non-finite values.
Results may differ from the reference program's by a relative error of at most 0.0045.
Values may be sent and summed in bfloat16 or wider, within the bound.
A program may use at most 64 MiB of HBM per device.

```python
import math
import jax
import jax.numpy as jnp
from jax import lax

DIM = 128
QT = 32
BUCKETS = 16
CENT_DEV = 4096
H = 256
HEADS = 4
FF = 1024
HEAD = 64
NCS = 4
NQ = 4
QROWS = 128
NDOCS = 128
PAD = 128
CAND = 64
NCENT = 16384


def draw_slot_counts(key, part):
    half_pad = PAD // 2

    def one_doc(doc_key):
        device_order = jax.random.permutation(jax.random.fold_in(doc_key, 1), NCS)
        offsets = jax.random.randint(jax.random.fold_in(doc_key, 2), (NCS // 2,), 0, half_pad + 1)
        offsets = offsets.at[0].set(half_pad)
        paired = jnp.stack([half_pad + offsets, half_pad - offsets], axis=1).reshape(NCS)
        return jnp.zeros((NCS,), jnp.int32).at[device_order].set(paired.astype(jnp.int32))
    doc_keys = jax.random.split(jax.random.fold_in(key, 5), NDOCS)
    return jax.vmap(one_doc)(doc_keys).T.astype(jnp.int32)


def draw_candidates(key, part):
    query_keys = jax.random.split(jax.random.fold_in(key, 3), NQ)

    def one_query(query_key):
        return jax.random.permutation(query_key, NDOCS)[:CAND]
    return jax.vmap(one_query)(query_keys).astype(jnp.int32)


def bounded_entries(key):
    unit = jax.random.uniform(key, (H, H), jnp.float32, -1.0, 1.0)
    return unit * math.sqrt(3.0 / H)


def head_factors(key):
    ladder = jnp.exp(jnp.linspace(0.0, math.log(4.0), HEADS)).astype(jnp.float32)
    order = jax.random.permutation(jax.random.fold_in(key, 17), HEADS)
    return jnp.repeat(ladder[order], HEAD)[None, :]


def draw_query_proj(key, part):
    entries = bounded_entries(jax.random.fold_in(key, 7))
    spread_part = 3.0 * entries * head_factors(key)
    return spread_part.astype(jnp.bfloat16)


def draw_key_proj(key, part):
    return bounded_entries(jax.random.fold_in(key, 11)).astype(jnp.bfloat16)


def place_ends(values, rng, smallest, high):
    place = [jax.random.randint(jax.random.fold_in(rng, axis), (), 0, length) for axis, length in enumerate(values.shape)]
    main_axis = values.shape.index(max(values.shape))
    next_to = place[:main_axis] + [(place[main_axis] + 1) % values.shape[main_axis]] + place[main_axis + 1:]
    return values.at[tuple(place)].set(smallest).at[tuple(next_to)].set(high)


def block_levels(stream_key, dims, pieces, smallest, top_value):
    def one(position, shards_of):
        draws = jax.random.uniform(jax.random.fold_in(jax.random.fold_in(stream_key, 6), position), (shards_of,), jnp.float32, smallest / len(pieces), top_value / len(pieces))
        return jnp.repeat(jnp.exp(draws), dims[position] // shards_of).reshape((-1,) + (1,) * (len(dims) - position - 1))

    factor_of = one(*pieces[0])
    for cut in pieces[1:]:
        factor_of = factor_of * one(*cut)
    return factor_of


def scatter_about(stream_key, dims, spread, bound, cuts=(), kind=jnp.bfloat16):
    array = spread * jax.random.normal(stream_key, dims, jnp.float32)
    if cuts:
        array = array * block_levels(stream_key, dims, cuts, -0.22, 0.18)
    return jnp.clip(array, -bound, bound).astype(kind)


def setup_inputs(seed: int = 0, part: int = 0) -> dict:
    splits = jax.random.split(jax.random.key(seed), 17)
    part_keys = jax.random.split(jax.random.fold_in(splits[16], part), 17)
    return {
        "queries": scatter_about(part_keys[0], (QROWS, DIM), 0.1, 0.6, ((0, 4),), jnp.float32),
        "token_codes": place_ends(jax.random.randint(part_keys[1], (NCS, NDOCS, PAD * DIM // 2), 0, 256), jax.random.fold_in(part_keys[1], 1), 0, 255).astype(jnp.int32),
        "centroid_ids": place_ends(jax.random.randint(part_keys[2], (NCS, NDOCS * PAD), 0, CENT_DEV), jax.random.fold_in(part_keys[2], 1), 0, CENT_DEV - 1).astype(jnp.int32),
        "slot_counts": draw_slot_counts(jax.random.fold_in(jax.random.fold_in(splits[16], part), 71), part),
        "centroids": scatter_about(splits[4], (NCENT, DIM), 0.5, 3.0, ((0, 4),)),
        "bucket_values": scatter_about(splits[5], (BUCKETS, DIM), 0.3, 1.5, (), jnp.float32),
        "candidates": draw_candidates(jax.random.fold_in(jax.random.fold_in(splits[16], part), 71), part),
        "input_proj": scatter_about(splits[7], (QT, H), QT ** -0.5, 1.0, (), jnp.float32),
        "gain_one": jnp.clip(1.0 + 0.1 * jax.random.normal(splits[8], (H,), jnp.float32), 0.5, 1.5),
        "query_proj": draw_query_proj(jax.random.fold_in(splits[16], 71), part),
        "key_proj": draw_key_proj(jax.random.fold_in(splits[16], 71), part),
        "value_proj": scatter_about(splits[11], (H, H), H ** -0.5, 0.375),
        "output_proj": scatter_about(splits[12], (H, H), H ** -0.5, 0.375),
        "gain_two": jnp.clip(1.0 + 0.1 * jax.random.normal(splits[13], (H,), jnp.float32), 0.5, 1.5),
        "up_proj": scatter_about(splits[14], (H, FF), H ** -0.5, 0.375),
        "down_proj": scatter_about(splits[15], (FF, H), FF ** -0.5, 0.1875),
    }


def dequantize(code_rows, cent_rows, centroid_table, bucket_table):
    lower = jnp.bitwise_and(code_rows, 15)
    upper = jnp.right_shift(code_rows, 4)
    nibbles = jnp.stack([lower, upper], axis=-1).reshape(code_rows.shape[0], -1)
    residual = jnp.zeros(nibbles.shape, jnp.float32)
    for level_id in range(bucket_table.shape[0]):
        residual = residual + jnp.where(nibbles == level_id, bucket_table[level_id][None, :], jnp.float32(0.0))
    anchor = jnp.take(centroid_table, cent_rows, axis=0).astype(jnp.float32)
    return (anchor + residual).astype(jnp.bfloat16)

def block_maxima(code_rows, cent_rows, live_counts, centroid_table, bucket_table, query_bf, pad_slots):
    embedded = dequantize(code_rows, cent_rows, centroid_table, bucket_table)
    scores = lax.dot_general(embedded, query_bf, (((1,), (1,)), ((), ())), preferred_element_type=jnp.float32)
    positions = jnp.arange(pad_slots, dtype=jnp.int32)
    live_slot = (positions[None, :] < live_counts[:, None]).reshape(-1)
    scores = jnp.where(live_slot[:, None], scores, jnp.float32(-1e+30))
    return lax.optimization_barrier(jnp.max(scores.reshape(live_counts.shape[0], pad_slots, scores.shape[1]), axis=1))

def rms_scale(values, gain):
    mean_square = lax.optimization_barrier(jnp.mean(values * values, axis=-1, keepdims=True))
    return (values * lax.rsqrt(mean_square + 1e-06) * gain).astype(jnp.bfloat16)

def widen(values):
    return lax.optimization_barrier(values).astype(jnp.float32)

def attend(query_heads, key_heads, value_heads):
    rows = query_heads.shape[0]
    query_four = widen(query_heads).reshape(rows, HEADS, HEAD)
    key_four = widen(key_heads).reshape(-1, HEADS, HEAD)
    value_four = widen(value_heads).reshape(-1, HEADS, HEAD)
    scores = jnp.einsum('qhd,khd->hqk', query_four, key_four) * HEAD ** (-0.5)
    peak = lax.optimization_barrier(jnp.max(scores, axis=-1, keepdims=True))
    expon = jnp.exp(scores - peak)
    summed = lax.optimization_barrier(jnp.sum(expon, axis=-1))
    weights = widen(expon.astype(jnp.bfloat16))
    product = jnp.einsum('hqk,khd->qhd', weights, value_four) / summed.T[:, :, None]
    return product.reshape(rows, H).astype(jnp.bfloat16)

def set_layer(features, input_proj, gain_one, query_proj, key_proj, value_proj, output_proj, gain_two, up_proj, down_proj):
    hidden_zero = jnp.dot(features, input_proj, precision=lax.Precision.HIGHEST)
    normed_one = rms_scale(hidden_zero, gain_one)
    query_heads = jnp.dot(normed_one, query_proj, preferred_element_type=jnp.float32).astype(jnp.bfloat16)
    key_heads = jnp.dot(normed_one, key_proj, preferred_element_type=jnp.float32).astype(jnp.bfloat16)
    value_heads = jnp.dot(normed_one, value_proj, preferred_element_type=jnp.float32).astype(jnp.bfloat16)
    attended = attend(query_heads, key_heads, value_heads)
    hidden_one = hidden_zero + jnp.dot(attended, output_proj, preferred_element_type=jnp.float32)
    normed_two = rms_scale(hidden_one, gain_two)
    inner = jax.nn.gelu(jnp.dot(normed_two, up_proj, preferred_element_type=jnp.float32)).astype(jnp.bfloat16)
    return hidden_one + jnp.dot(inner, down_proj, preferred_element_type=jnp.float32)

def reference(queries, token_codes, centroid_ids, slot_counts, centroids, bucket_values, candidates, input_proj, gain_one, query_proj, key_proj, value_proj, output_proj, gain_two, up_proj, down_proj):
    query_bf = queries.astype(jnp.bfloat16)
    block_docs = math.gcd(NDOCS, max(1, 2048 // PAD))
    block_count = NDOCS // block_docs
    code_view = token_codes.reshape(NCS, block_count, block_docs * PAD, DIM // 2)
    cent_view = centroid_ids.reshape(NCS, block_count, block_docs * PAD)
    count_view = slot_counts.reshape(NCS, block_count, block_docs)
    centroid_view = centroids.reshape(NCS, CENT_DEV, DIM)

    def one_block(block_id):
        running_best = jnp.full((block_docs, QROWS), -1e+30, jnp.float32)
        for member in range(NCS):
            running_best = jnp.maximum(running_best, block_maxima(code_view[member, block_id], cent_view[member, block_id], count_view[member, block_id], centroid_view[member], bucket_values, query_bf, PAD))
        return running_best
    maxima = lax.map(one_block, jnp.arange(block_count, dtype=jnp.int32)).reshape(NDOCS, QROWS)
    per_query = maxima.reshape(NDOCS, NQ, QT).transpose(1, 0, 2)
    features = jax.vmap(lambda table, row_ids: jnp.take(table, row_ids, axis=0))(per_query, candidates)

    def one_query(query_features):
        return set_layer(query_features, input_proj, gain_one, query_proj, key_proj, value_proj, output_proj, gain_two, up_proj, down_proj)
    return lax.map(one_query, features)
```

```python
import functools

import jax
import jax.numpy as jnp
from jax import lax
from jax.experimental import pallas as pl
from jax.experimental.pallas import tpu as pltpu
from jax.sharding import PartitionSpec as P

DIM = 128
QT = 32
H = 256
HEADS = 4
HEAD = 64
F32 = jnp.float32
BF16 = jnp.bfloat16
NT = (((1,), (1,)), ((), ()))
AXES = ("docs", "cent", "sub")


def iota(shape, axis):
    return lax.broadcasted_iota(jnp.int32, shape, axis)


def column(row):
    n = row.shape[1]
    wide = jnp.broadcast_to(row.astype(F32), (n, n))
    return jnp.sum(jnp.where(iota((n, n), 0) == iota((n, n), 1), wide, 0.0), axis=1, keepdims=True)


def wrap(value, size):
    return value & (size - 1) if size & (size - 1) == 0 else lax.rem(value, size)


def shift(value, size):
    return value >> (size.bit_length() - 1) if size & (size - 1) == 0 else lax.div(value, size)


def lookup(table, index):
    numbers = lax.GatherDimensionNumbers(
        offset_dims=(),
        collapsed_slice_dims=(0,),
        start_index_map=(0,),
        operand_batching_dims=(1,),
        start_indices_batching_dims=(1,),
    )
    return lax.gather(
        table,
        index[..., None],
        numbers,
        slice_sizes=(1, 1),
        mode=lax.GatherScatterMode.PROMISE_IN_BOUNDS,
    )


def spread(dim_of_lane):
    return (iota((DIM, DIM), 0) == dim_of_lane).astype(F32).astype(BF16)


def mm(a, b):
    return jnp.dot(a, b, preferred_element_type=F32)


def rms_scale(values, gain):
    mean_square = jnp.mean(values * values, axis=-1, keepdims=True)
    return (values * lax.rsqrt(mean_square + 1e-06) * gain).astype(BF16)


def kernel(
    sizes,
    queries_hbm,
    codes_hbm,
    ids_hbm,
    counts_hbm,
    centroids,
    buckets_hbm,
    candidates_hbm,
    input_proj_hbm,
    gain_one_hbm,
    query_proj,
    key_proj,
    value_proj,
    output_proj,
    gain_two_hbm,
    up_proj,
    down_proj,
    out,
    queries,
    ids,
    counts,
    buckets,
    candidates,
    input_proj,
    gain_one,
    gain_two,
    codes,
    cent_bf,
    table,
    embed,
    q_all,
    outbox,
    inbox,
    normed,
    hidden,
    wq,
    wk,
    wv,
    wo,
    wu,
    wd,
    load_sem,
    q_send,
    q_recv,
    b_send,
    b_recv,
):
    n_docs, n_cent, n_sub = sizes
    members = n_cent * n_sub
    total = n_docs * members
    docs_local = codes.shape[0]
    pad = codes.shape[1] * 2 // DIM
    tiles, pairs = docs_local // 8, pad // 2
    rows = docs_local // 4
    cand = candidates.shape[1]
    mine = cand // members

    z = lax.axis_index("docs")
    member = lax.axis_index("cent") * n_sub + lax.axis_index("sub")
    me = z * members + member

    def place(flat):
        return {
            "docs": shift(flat, members),
            "cent": shift(wrap(flat, members), n_sub),
            "sub": wrap(flat, n_sub),
        }

    def each(count, body):
        def step(i, carry):
            body(i)
            return carry

        lax.fori_loop(0, count, step, 0, unroll=count <= 16)

    parts = 4
    cent_rows = centroids.shape[0] // parts
    doc_rows = docs_local // parts
    cent_pieces = [
        (centroids.at[i * cent_rows : (i + 1) * cent_rows], cent_bf.at[i * cent_rows : (i + 1) * cent_rows])
        for i in range(parts)
    ]
    code_pieces = [
        (codes_hbm.at[0, i * doc_rows : (i + 1) * doc_rows], codes.at[i * doc_rows : (i + 1) * doc_rows])
        for i in range(parts)
    ]
    small = [(buckets_hbm, buckets), (counts_hbm, counts), (candidates_hbm, candidates)]
    late = [
        (input_proj_hbm, input_proj),
        (gain_one_hbm, gain_one),
        (gain_two_hbm, gain_two),
        (query_proj, wq),
        (key_proj, wk),
        (value_proj, wv),
        (output_proj, wo),
        (up_proj, wu),
        (down_proj, wd),
    ]
    order = [(ids_hbm, ids), (queries_hbm, queries), *small, *cent_pieces, *code_pieces, *late]
    pulls = [
        pltpu.make_async_copy(src, dst, load_sem.at[i]) for i, (src, dst) in enumerate(order)
    ]
    ids_pull, query_pull = pulls[0:2]
    small_pulls, cent_pulls = pulls[2:5], pulls[5 : 5 + parts]
    code_pulls, late_pulls = pulls[5 + parts : 5 + 2 * parts], pulls[5 + 2 * parts :]
    for pull in (*pulls[: 5 + 2 * parts],):
        pull.start()
    barrier = pltpu.get_barrier_semaphore()
    each(
        total - 1,
        lambda i: pl.semaphore_signal(barrier, inc=1, device_id=place(wrap(me + i + 1, total))),
    )
    for pull in small_pulls:
        pull.wait()

    lane = iota((DIM, DIM), 1)
    half = lane % 64
    bucket_bf = buckets[...].astype(BF16)
    even = mm(bucket_bf, spread(2 * half))
    odd = mm(bucket_bf, spread(2 * half + 1))
    live = column(counts[...])
    cand_col = column(candidates[...])
    tabs = (even[0:8], even[8:16], odd[0:8], odd[8:16])

    def pick(low, high, index, upper):
        return jnp.where(
            upper,
            lookup(high, index),
            lookup(low, index),
        )

    def loop(first, last, body):
        def step(i, carry):
            body(i)
            return carry

        lax.fori_loop(first, last, step, 0)

    block = 256

    def widen(i):
        at = pl.ds(pl.multiple_of(i * block, block), block)
        table[at, :] = cent_bf[at, :].astype(F32)

    for i in range(parts):
        cent_pulls[i].wait()
        loop(i * cent_rows // block, (i + 1) * cent_rows // block, widen)
    sub = iota((8, DIM), 0)
    none = shift(me, 1 << 20)
    steps = [none + s * pad for s in range(8)]

    group = 8 if pairs % 8 == 0 else 2

    def tile(t):
        def pair(k):
            start = pl.multiple_of(t * (8 * pad) + k * (2 * group), 2 * group)
            for u in range(0, group, 2):
                at = pl.ds(pl.multiple_of(t * (pairs * 8) + k * (8 * group) + u * 8, 16), 16)
                lows, highs = [], []
                for v in range(u, u + 2):
                    word = codes[
                        pl.ds(pl.multiple_of(t * 8, 8), 8),
                        pl.ds(pl.multiple_of(k * (group * DIM) + v * DIM, DIM), DIM),
                    ]
                    lows.append(pick(tabs[0], tabs[1], word & 7, (word & 8) != 0))
                    highs.append(pick(tabs[2], tabs[3], (word >> 4) & 7, word >= 128))
                embed[at, 2 * DIM : 3 * DIM] = jnp.concatenate(lows, axis=0).astype(BF16)
                embed[at, 3 * DIM : 4 * DIM] = jnp.concatenate(highs, axis=0).astype(BF16)
                for h in range(2):
                    both = []
                    for v in range(u, u + 2):
                        acc = None
                        near = ids.at[0, pl.ds(start + (2 * v + h), 7 * pad + 1)]
                        for s in range(8):
                            slot = near[steps[s]]
                            row = jnp.broadcast_to(table[pl.ds(slot, 1), :], (8, DIM))
                            acc = row if acc is None else jnp.where(sub == s, row, acc)
                        both.append(acc)
                    embed[at, h * DIM : (h + 1) * DIM] = jnp.concatenate(both, axis=0).astype(BF16)

        loop(0, pairs // group, pair)

    def q_copy(i):
        to = wrap(member + i + 1, members)
        return pltpu.make_async_remote_copy(
            src_ref=queries,
            dst_ref=q_all.at[member],
            send_sem=q_send.at[i],
            recv_sem=q_recv.at[member],
            device_id={"cent": shift(to, n_sub), "sub": wrap(to, n_sub)},
        )

    ids_pull.wait()
    for i in range(parts):
        code_pulls[i].wait()
        loop(i * tiles // parts, (i + 1) * tiles // parts, tile)
        if i == 0:
            query_pull.wait()
            pl.semaphore_wait(barrier, total - 1)
            each(members - 1, lambda i: q_copy(i).start())
            for pull in late_pulls:
                pull.start()

    def q_wait(i):
        source = wrap(member + i + 1, members)
        pltpu.make_async_remote_copy(
            src_ref=queries,
            dst_ref=q_all.at[source],
            send_sem=q_send.at[i],
            recv_sem=q_recv.at[source],
            device_id={"cent": shift(source, n_sub), "sub": wrap(source, n_sub)},
        ).wait()

    each(members - 1, q_wait)
    q_all[member] = queries[...]
    q_rows = members * QT
    splits = q_rows // DIM
    zero = jnp.zeros((DIM, DIM), BF16)
    spreads = [spread(2 * lane + o) for o in (0, -DIM, 1, 1 - DIM)]
    chunk = pairs
    for n in range(splits):
        q_bf = q_all[n * (DIM // QT) : (n + 1) * (DIM // QT)].reshape(DIM, DIM).astype(BF16)
        le, ue, lo, uo = [mm(q_bf, p).astype(BF16) for p in spreads]
        weight = jnp.concatenate(
            [
                jnp.concatenate([q_bf, zero, le, lo], axis=1),
                jnp.concatenate([zero, q_bf, ue, uo], axis=1),
            ],
            axis=0,
        )
        for t in range(tiles):
            live_t = jnp.broadcast_to(live[t * 8 : t * 8 + 8], (8, DIM))
            best = jnp.full((8, DIM), -1e30, F32)
            for k in range(0, pairs, chunk):
                at = (t * pairs + k) * 8
                scores = lax.dot_general(
                    embed[at : at + chunk * 8, :], weight, NT, preferred_element_type=F32
                )
                for u in range(chunk):
                    for h in range(2):
                        part = scores[u * 8 : u * 8 + 8, h * DIM : (h + 1) * DIM]
                        part = jnp.where(live_t > 2.0 * (k + u) + h, part, -1e30)
                        best = jnp.maximum(best, part)
            for g in range(4):
                to = t % 4
                moved = best if g == to else pltpu.roll(best, (to - g) * QT % DIM, 1)
                outbox[n * 4 + g, t // 4 * 8 : t // 4 * 8 + 8, to * QT : (to + 1) * QT] = moved[
                    :, to * QT : (to + 1) * QT
                ]

    def b_copy(i, flat, slot):
        return pltpu.make_async_remote_copy(
            src_ref=outbox.at[shift(flat, members)],
            dst_ref=inbox.at[slot],
            send_sem=b_send.at[i],
            recv_sem=b_recv.at[slot],
            device_id=place(flat),
        )

    def b_start(i):
        b_copy(i, i + jnp.where(i >= me, 1, 0), me).start()

    each(total - 1, b_start)
    inbox[me] = outbox[z]

    docs_all = n_docs * docs_local
    c_int = cand_col.astype(jnp.int32)
    within = c_int % docs_local
    row_of = c_int // docs_local * rows + within // 32 * 8 + within % 8
    lanes_of = within // 8 % 4
    one_hot = (iota((cand, docs_all // 4), 1) == row_of).astype(F32)
    for pull in late_pulls:
        pull.wait()
    in_four = jnp.concatenate([input_proj[...]] * 4, axis=0)

    def b_wait(i):
        flat = wrap(me + i + 1, total)
        b_copy(i, flat, flat).wait()

    each(total - 1, b_wait)
    maxima = jnp.concatenate(
        [
            functools.reduce(jnp.maximum, [inbox[d * members + m] for m in range(members)])
            for d in range(n_docs)
        ],
        axis=0,
    )
    high = lax.Precision.HIGHEST
    picked = jnp.dot(one_hot, maxima, precision=high, preferred_element_type=F32)
    picked = jnp.where(iota((cand, DIM), 1) // QT == lanes_of, picked, 0.0)
    all_hidden = jnp.dot(picked, in_four, precision=high, preferred_element_type=F32)
    all_normed = rms_scale(all_hidden, gain_one[...])
    hidden[...] = all_hidden
    normed[...] = all_normed.astype(F32)
    here = pl.ds(pl.multiple_of(member * mine, 8), mine)
    hidden_zero = hidden[here, :]
    q_heads = mm(normed[here, :].astype(BF16), wq[...]).astype(BF16)
    k_heads = mm(all_normed, wk[...]).astype(BF16)
    v_heads = mm(all_normed, wv[...]).astype(BF16)
    head_of = iota((mine, H), 1) // HEAD
    q_stack = jnp.concatenate(
        [jnp.where(head_of == h, q_heads.astype(F32), 0.0) for h in range(HEADS)], axis=0
    ).astype(BF16)
    att = lax.dot_general(q_stack, k_heads, NT, preferred_element_type=F32) * HEAD ** (-0.5)
    expon = jnp.exp(att - jnp.max(att, axis=-1, keepdims=True))
    mixed = mm(expon.astype(BF16), v_heads) / jnp.sum(expon, axis=-1, keepdims=True)
    attended = functools.reduce(
        jnp.add,
        [
            jnp.where(head_of == h, mixed[h * mine : (h + 1) * mine], 0.0)
            for h in range(HEADS)
        ],
    ).astype(BF16)
    hidden_one = hidden_zero + mm(attended, wo[...])
    normed_two = rms_scale(hidden_one, gain_two[...])
    inner = jax.nn.gelu(mm(normed_two, wu[...])).astype(BF16)
    out[0] = hidden_one + mm(inner, wd[...])


def on_device(sizes, *args):
    (queries, codes, ids, counts, centroids, buckets, candidates, input_proj, gain_one) = args[:9]
    (query_proj, key_proj, value_proj, output_proj, gain_two, up_proj, down_proj) = args[9:]
    n_docs, n_cent, n_sub = sizes
    members = n_cent * n_sub
    total = n_docs * members
    docs_local, width = codes.shape[1:]
    cand = candidates.shape[1]
    slots = docs_local * width * 2 // DIM
    vmem = pl.BlockSpec(memory_space=pltpu.VMEM)
    hbm = pl.BlockSpec(memory_space=pl.ANY)
    weights = (query_proj, key_proj, value_proj, output_proj, up_proj, down_proj)
    return pl.pallas_call(
        functools.partial(kernel, sizes),
        out_shape=pltpu.VMEM((1, cand // members, H), F32),
        in_specs=[hbm] * 16,
        out_specs=vmem,
        scratch_shapes=[
            pltpu.VMEM(queries.shape, F32),
            pltpu.SMEM(ids.shape, jnp.int32),
            pltpu.VMEM(counts.shape, jnp.int32),
            pltpu.VMEM(buckets.shape, F32),
            pltpu.VMEM(candidates.shape, jnp.int32),
            pltpu.VMEM(input_proj.shape, F32),
            pltpu.VMEM((1, H), F32),
            pltpu.VMEM((1, H), F32),
            pltpu.VMEM((docs_local, width), jnp.int32),
            pltpu.VMEM(centroids.shape, BF16),
            pltpu.VMEM(centroids.shape, F32),
            pltpu.VMEM((slots // 2, 4 * DIM), BF16),
            pltpu.VMEM((members, QT, DIM), F32),
            pltpu.VMEM((n_docs, docs_local // 4, DIM), F32),
            pltpu.VMEM((total, docs_local // 4, DIM), F32),
            pltpu.VMEM((cand, H), F32),
            pltpu.VMEM((cand, H), F32),
            *[pltpu.VMEM(w.shape, BF16) for w in weights],
            pltpu.SemaphoreType.DMA((22,)),
            pltpu.SemaphoreType.DMA((members,)),
            pltpu.SemaphoreType.DMA((members,)),
            pltpu.SemaphoreType.DMA((total,)),
            pltpu.SemaphoreType.DMA((total,)),
        ],
        compiler_params=pltpu.CompilerParams(collective_id=0, has_side_effects=True),
    )(
        queries,
        codes,
        ids,
        counts,
        centroids,
        buckets,
        candidates,
        input_proj,
        gain_one.reshape(1, H),
        query_proj,
        key_proj,
        value_proj,
        output_proj,
        gain_two.reshape(1, H),
        up_proj,
        down_proj,
    )


def solution(mesh):
    in_specs = (
        P(("groups", "cent", "sub"), None),
        P(("cent", "sub"), ("groups", "docs"), None),
        P(("cent", "sub"), ("groups", "docs")),
        P(("cent", "sub"), ("groups", "docs")),
        P(("cent", "sub"), None),
        P(),
        P(("groups", "docs"), None),
        P(),
        P(),
        P(),
        P(),
        P(),
        P(),
        P(),
        P(),
        P(),
    )
    out_specs = P(("groups", "docs"), ("cent", "sub"), None)
    sizes = tuple(mesh.shape[name] for name in AXES)
    return jax.shard_map(
        functools.partial(on_device, sizes),
        mesh=mesh,
        in_specs=in_specs,
        out_specs=out_specs,
        check_vma=False,
    )
```

```python
import functools

import jax
import jax.numpy as jnp
from jax import lax
from jax.experimental import pallas as pl
from jax.experimental.pallas import tpu as pltpu
from jax.sharding import PartitionSpec as P

DIM = 128
QT = 32
H = 256
HEADS = 4
HEAD = 64
F32 = jnp.float32
BF16 = jnp.bfloat16
NT = (((1,), (1,)), ((), ()))
AXES = ("docs", "cent", "sub")


def iota(shape, axis):
    return lax.broadcasted_iota(jnp.int32, shape, axis)


def column(row):
    n = row.shape[1]
    wide = jnp.broadcast_to(row.astype(F32), (n, n))
    return jnp.sum(jnp.where(iota((n, n), 0) == iota((n, n), 1), wide, 0.0), axis=1, keepdims=True)


def wrap(value, size):
    return value & (size - 1) if size & (size - 1) == 0 else lax.rem(value, size)


def shift(value, size):
    return value >> (size.bit_length() - 1) if size & (size - 1) == 0 else lax.div(value, size)


def lookup(table, index, axis):
    numbers = lax.GatherDimensionNumbers(
        offset_dims=(),
        collapsed_slice_dims=(axis,),
        start_index_map=(axis,),
        operand_batching_dims=(1 - axis,),
        start_indices_batching_dims=(1 - axis,),
    )
    return lax.gather(
        table,
        index[..., None],
        numbers,
        slice_sizes=(1, 1),
        mode=lax.GatherScatterMode.PROMISE_IN_BOUNDS,
    )


def halves(values):
    high = values.astype(BF16)
    return high, (values - high.astype(F32)).astype(BF16)


def mm(a, b):
    return jnp.dot(a, b, preferred_element_type=F32)


def rms_scale(values, gain):
    mean_square = jnp.mean(values * values, axis=-1, keepdims=True)
    return (values * lax.rsqrt(mean_square + 1e-06) * gain).astype(BF16)


def kernel(
    sizes,
    queries_hbm,
    codes_hbm,
    ids_hbm,
    counts_hbm,
    centroids,
    buckets_hbm,
    candidates_hbm,
    input_proj_hbm,
    gain_one_hbm,
    query_proj,
    key_proj,
    value_proj,
    output_proj,
    gain_two_hbm,
    up_proj,
    down_proj,
    out,
    queries,
    q_own,
    ids,
    counts,
    buckets,
    candidates,
    input_proj,
    gain_one,
    gain_two,
    codes,
    cent_bf,
    table,
    embed,
    q_all,
    outbox,
    inbox,
    normed,
    hidden,
    wq,
    wk,
    wv,
    wo,
    wu,
    wd,
    load_sem,
    q_send,
    q_recv,
    b_send,
    b_recv,
):
    n_docs, n_cent, n_sub = sizes
    members = n_cent * n_sub
    total = n_docs * members
    docs_local = codes.shape[0]
    pad = codes.shape[1] * 2 // DIM
    tiles, pairs = docs_local // 8, pad // 2
    rows = docs_local // 4
    cand = candidates.shape[1]
    mine = cand // members

    z = lax.axis_index("docs")
    member = lax.axis_index("cent") * n_sub + lax.axis_index("sub")
    me = z * members + member

    def place(flat):
        return {
            "docs": shift(flat, members),
            "cent": shift(wrap(flat, members), n_sub),
            "sub": wrap(flat, n_sub),
        }

    def each(count, body):
        def step(i, carry):
            body(i)
            return carry

        lax.fori_loop(0, count, step, 0, unroll=count <= 16)

    parts = 4
    cent_rows = centroids.shape[0] // parts
    doc_rows = docs_local // parts
    cent_pieces = [
        (centroids.at[i * cent_rows : (i + 1) * cent_rows], cent_bf.at[i * cent_rows : (i + 1) * cent_rows])
        for i in range(parts)
    ]
    code_pieces = [
        (codes_hbm.at[0, i * doc_rows : (i + 1) * doc_rows], codes.at[i * doc_rows : (i + 1) * doc_rows])
        for i in range(parts)
    ]
    small = [(buckets_hbm, buckets), (counts_hbm, counts), (candidates_hbm, candidates)]
    late = [
        (input_proj_hbm, input_proj),
        (gain_one_hbm, gain_one),
        (gain_two_hbm, gain_two),
        (query_proj, wq),
        (key_proj, wk),
        (value_proj, wv),
        (output_proj, wo),
        (up_proj, wu),
        (down_proj, wd),
    ]
    order = [(ids_hbm, ids), (queries_hbm, queries), *small, *cent_pieces, *code_pieces, *late]
    pulls = [
        pltpu.make_async_copy(src, dst, load_sem.at[i]) for i, (src, dst) in enumerate(order)
    ]
    ids_pull, query_pull = pulls[0:2]
    small_pulls, cent_pulls = pulls[2:5], pulls[5 : 5 + parts]
    code_pulls, late_pulls = pulls[5 + parts : 5 + 2 * parts], pulls[5 + 2 * parts :]
    for pull in (*pulls[: 5 + 2 * parts],):
        pull.start()
    barrier = pltpu.get_barrier_semaphore()
    each(
        total - 1,
        lambda i: pl.semaphore_signal(barrier, inc=1, device_id=place(wrap(me + i + 1, total))),
    )
    for pull in small_pulls:
        pull.wait()

    live = column(counts[...])
    cand_col = column(candidates[...])
    low_levels, high_levels = buckets[0:8, :], buckets[8:16, :]
    lane = iota((8, DIM), 1)
    words = [(lane >> 1) + 64 * h for h in range(2)]
    nibble = (lane & 1) * 4

    def residual(word, h):
        code = lookup(word, words[h], 1) >> nibble
        level = code & 7
        return jnp.where(
            (code & 8) != 0,
            lookup(high_levels, level, 0),
            lookup(low_levels, level, 0),
        )

    def loop(first, last, body):
        def step(i, carry):
            body(i)
            return carry

        lax.fori_loop(first, last, step, 0)

    block = 256

    def widen(i):
        at = pl.ds(pl.multiple_of(i * block, block), block)
        table[at, :] = cent_bf[at, :].astype(F32)

    for i in range(parts):
        cent_pulls[i].wait()
        loop(i * cent_rows // block, (i + 1) * cent_rows // block, widen)
    sub = iota((8, DIM), 0)
    none = shift(me, 1 << 20)
    steps = [none + s * pad for s in range(8)]

    group = 8 if pairs % 8 == 0 else 2

    def tile(t):
        def pair(k):
            start = pl.multiple_of(t * (8 * pad) + k * (2 * group), 2 * group)
            for u in range(0, group, 2):
                at = pl.ds(pl.multiple_of(t * (pairs * 8) + k * (8 * group) + u * 8, 16), 16)
                both = [[], []]
                for v in range(u, u + 2):
                    word = codes[
                        pl.ds(pl.multiple_of(t * 8, 8), 8),
                        pl.ds(pl.multiple_of(k * (group * DIM) + v * DIM, DIM), DIM),
                    ]
                    for h in range(2):
                        acc = None
                        near = ids.at[0, pl.ds(start + (2 * v + h), 7 * pad + 1)]
                        for s in range(8):
                            slot = near[steps[s]]
                            row = jnp.broadcast_to(table[pl.ds(slot, 1), :], (8, DIM))
                            acc = row if acc is None else jnp.where(sub == s, row, acc)
                        both[h].append(acc + residual(word, h))
                for h in range(2):
                    embed[at, h * DIM : (h + 1) * DIM] = jnp.concatenate(both[h], axis=0).astype(BF16)

        loop(0, pairs // group, pair)

    def q_copy(i):
        to = wrap(member + i + 1, members)
        return pltpu.make_async_remote_copy(
            src_ref=q_own,
            dst_ref=q_all.at[member],
            send_sem=q_send.at[i],
            recv_sem=q_recv.at[member],
            device_id={"cent": shift(to, n_sub), "sub": wrap(to, n_sub)},
        )

    ids_pull.wait()
    query_pull.wait()
    q_own[...] = queries[...].astype(BF16)
    for i in range(parts):
        code_pulls[i].wait()
        loop(i * tiles // parts, (i + 1) * tiles // parts, tile)
        if i == 1:
            pl.semaphore_wait(barrier, total - 1)
            each(members - 1, lambda i: q_copy(i).start())
            for pull in late_pulls:
                pull.start()

    def q_wait(i):
        source = wrap(member + i + 1, members)
        pltpu.make_async_remote_copy(
            src_ref=q_own,
            dst_ref=q_all.at[source],
            send_sem=q_send.at[i],
            recv_sem=q_recv.at[source],
            device_id={"cent": shift(source, n_sub), "sub": wrap(source, n_sub)},
        ).wait()

    each(members - 1, q_wait)
    q_all[member] = q_own[...]
    q_rows = members * QT
    splits = q_rows // DIM
    zero = jnp.zeros((DIM, DIM), BF16)
    chunk = pairs
    for n in range(splits):
        q_bf = q_all[n * (DIM // QT) : (n + 1) * (DIM // QT)].reshape(DIM, DIM)
        weight = jnp.concatenate(
            [
                jnp.concatenate([q_bf, zero], axis=1),
                jnp.concatenate([zero, q_bf], axis=1),
            ],
            axis=0,
        )
        for t in range(tiles):
            live_t = jnp.broadcast_to(live[t * 8 : t * 8 + 8], (8, DIM))
            best = jnp.full((8, DIM), -1e30, F32)
            for k in range(0, pairs, chunk):
                at = (t * pairs + k) * 8
                scores = lax.dot_general(
                    embed[at : at + chunk * 8, :], weight, NT, preferred_element_type=F32
                )
                for u in range(chunk):
                    for h in range(2):
                        part = scores[u * 8 : u * 8 + 8, h * DIM : (h + 1) * DIM]
                        part = jnp.where(live_t > 2.0 * (k + u) + h, part, -1e30)
                        best = jnp.maximum(best, part)
            for g in range(4):
                to = t % 4
                moved = best if g == to else pltpu.roll(best, (to - g) * QT % DIM, 1)
                outbox[n * 4 + g, t // 4 * 8 : t // 4 * 8 + 8, to * QT : (to + 1) * QT] = moved[
                    :, to * QT : (to + 1) * QT
                ]

    def b_copy(i, flat, slot):
        return pltpu.make_async_remote_copy(
            src_ref=outbox.at[shift(flat, members)],
            dst_ref=inbox.at[slot],
            send_sem=b_send.at[i],
            recv_sem=b_recv.at[slot],
            device_id=place(flat),
        )

    def b_start(i):
        b_copy(i, i + jnp.where(i >= me, 1, 0), me).start()

    each(total - 1, b_start)
    inbox[me] = outbox[z]

    docs_all = n_docs * docs_local
    c_int = cand_col.astype(jnp.int32)
    within = c_int % docs_local
    row_of = c_int // docs_local * rows + within // 32 * 8 + within % 8
    lanes_of = within // 8 % 4
    one_hot = (iota((cand, docs_all // 4), 1) == row_of).astype(F32).astype(BF16)
    one_hot = jnp.concatenate([one_hot, one_hot], axis=1)
    for pull in late_pulls:
        pull.wait()
    in_high, in_low = halves(jnp.concatenate([input_proj[...]] * 4, axis=0))
    in_four = jnp.concatenate([in_high, in_high, in_low], axis=0)

    def b_wait(i):
        flat = wrap(me + i + 1, total)
        b_copy(i, flat, flat).wait()

    each(total - 1, b_wait)
    maxima = jnp.concatenate(
        [
            functools.reduce(jnp.maximum, [inbox[d * members + m] for m in range(members)])
            for d in range(n_docs)
        ],
        axis=0,
    )
    picked = mm(one_hot, jnp.concatenate(halves(maxima), axis=0))
    picked = jnp.where(iota((cand, DIM), 1) // QT == lanes_of, picked, 0.0)
    high, low = halves(picked)
    all_hidden = mm(jnp.concatenate([high, low, high], axis=1), in_four)
    all_normed = rms_scale(all_hidden, gain_one[...])
    hidden[...] = all_hidden
    normed[...] = all_normed.astype(F32)
    here = pl.ds(pl.multiple_of(member * mine, 8), mine)
    hidden_zero = hidden[here, :]
    q_heads = mm(normed[here, :].astype(BF16), wq[...]).astype(BF16)
    k_heads = mm(all_normed, wk[...]).astype(BF16)
    v_heads = mm(all_normed, wv[...]).astype(BF16)
    head_of = iota((mine, H), 1) // HEAD
    q_stack = jnp.concatenate(
        [jnp.where(head_of == h, q_heads.astype(F32), 0.0) for h in range(HEADS)], axis=0
    ).astype(BF16)
    att = lax.dot_general(q_stack, k_heads, NT, preferred_element_type=F32) * HEAD ** (-0.5)
    expon = jnp.exp(att - jnp.max(att, axis=-1, keepdims=True))
    mixed = mm(expon.astype(BF16), v_heads) / jnp.sum(expon, axis=-1, keepdims=True)
    attended = functools.reduce(
        jnp.add,
        [
            jnp.where(head_of == h, mixed[h * mine : (h + 1) * mine], 0.0)
            for h in range(HEADS)
        ],
    ).astype(BF16)
    hidden_one = hidden_zero + mm(attended, wo[...])
    normed_two = rms_scale(hidden_one, gain_two[...])
    inner = jax.nn.gelu(mm(normed_two, wu[...])).astype(BF16)
    out[0] = hidden_one + mm(inner, wd[...])


def on_device(sizes, *args):
    (queries, codes, ids, counts, centroids, buckets, candidates, input_proj, gain_one) = args[:9]
    (query_proj, key_proj, value_proj, output_proj, gain_two, up_proj, down_proj) = args[9:]
    n_docs, n_cent, n_sub = sizes
    members = n_cent * n_sub
    total = n_docs * members
    docs_local, width = codes.shape[1:]
    cand = candidates.shape[1]
    slots = docs_local * width * 2 // DIM
    vmem = pl.BlockSpec(memory_space=pltpu.VMEM)
    hbm = pl.BlockSpec(memory_space=pl.ANY)
    weights = (query_proj, key_proj, value_proj, output_proj, up_proj, down_proj)
    return pl.pallas_call(
        functools.partial(kernel, sizes),
        out_shape=pltpu.VMEM((1, cand // members, H), F32),
        in_specs=[hbm] * 16,
        out_specs=vmem,
        scratch_shapes=[
            pltpu.VMEM(queries.shape, F32),
            pltpu.VMEM(queries.shape, BF16),
            pltpu.SMEM(ids.shape, jnp.int32),
            pltpu.VMEM(counts.shape, jnp.int32),
            pltpu.VMEM(buckets.shape, F32),
            pltpu.VMEM(candidates.shape, jnp.int32),
            pltpu.VMEM(input_proj.shape, F32),
            pltpu.VMEM((1, H), F32),
            pltpu.VMEM((1, H), F32),
            pltpu.VMEM((docs_local, width), jnp.int32),
            pltpu.VMEM(centroids.shape, BF16),
            pltpu.VMEM(centroids.shape, F32),
            pltpu.VMEM((slots // 2, 2 * DIM), BF16),
            pltpu.VMEM((members, QT, DIM), BF16),
            pltpu.VMEM((n_docs, docs_local // 4, DIM), F32),
            pltpu.VMEM((total, docs_local // 4, DIM), F32),
            pltpu.VMEM((cand, H), F32),
            pltpu.VMEM((cand, H), F32),
            *[pltpu.VMEM(w.shape, BF16) for w in weights],
            pltpu.SemaphoreType.DMA((22,)),
            pltpu.SemaphoreType.DMA((members,)),
            pltpu.SemaphoreType.DMA((members,)),
            pltpu.SemaphoreType.DMA((total,)),
            pltpu.SemaphoreType.DMA((total,)),
        ],
        compiler_params=pltpu.CompilerParams(collective_id=0, has_side_effects=True),
    )(
        queries,
        codes,
        ids,
        counts,
        centroids,
        buckets,
        candidates,
        input_proj,
        gain_one.reshape(1, H),
        query_proj,
        key_proj,
        value_proj,
        output_proj,
        gain_two.reshape(1, H),
        up_proj,
        down_proj,
    )


def solution(mesh):
    in_specs = (
        P(("groups", "cent", "sub"), None),
        P(("cent", "sub"), ("groups", "docs"), None),
        P(("cent", "sub"), ("groups", "docs")),
        P(("cent", "sub"), ("groups", "docs")),
        P(("cent", "sub"), None),
        P(),
        P(("groups", "docs"), None),
        P(),
        P(),
        P(),
        P(),
        P(),
        P(),
        P(),
        P(),
        P(),
    )
    out_specs = P(("groups", "docs"), ("cent", "sub"), None)
    sizes = tuple(mesh.shape[name] for name in AXES)
    return jax.shard_map(
        functools.partial(on_device, sizes),
        mesh=mesh,
        in_specs=in_specs,
        out_specs=out_specs,
        check_vma=False,
    )
```

```python
import functools

import jax
import jax.numpy as jnp
from jax import lax
from jax.experimental import pallas as pl
from jax.experimental.pallas import tpu as pltpu
from jax.sharding import PartitionSpec as P

DIM = 128
QT = 32
H = 256
HEADS = 4
HEAD = 64
F32 = jnp.float32
BF16 = jnp.bfloat16
NT = (((1,), (1,)), ((), ()))
AXES = ("docs", "cent", "sub")


def iota(shape, axis):
    return lax.broadcasted_iota(jnp.int32, shape, axis)


def column(row):
    n = row.shape[1]
    wide = jnp.broadcast_to(row.astype(F32), (n, n))
    return jnp.sum(jnp.where(iota((n, n), 0) == iota((n, n), 1), wide, 0.0), axis=1, keepdims=True)


def wrap(value, size):
    return value & (size - 1) if size & (size - 1) == 0 else lax.rem(value, size)


def shift(value, size):
    return value >> (size.bit_length() - 1) if size & (size - 1) == 0 else lax.div(value, size)


def lookup(table, index, axis):
    numbers = lax.GatherDimensionNumbers(
        offset_dims=(),
        collapsed_slice_dims=(axis,),
        start_index_map=(axis,),
        operand_batching_dims=(1 - axis,),
        start_indices_batching_dims=(1 - axis,),
    )
    return lax.gather(
        table,
        index[..., None],
        numbers,
        slice_sizes=(1, 1),
        mode=lax.GatherScatterMode.PROMISE_IN_BOUNDS,
    )


def halves(values):
    high = values.astype(BF16)
    return high, (values - high.astype(F32)).astype(BF16)


def mm(a, b):
    return jnp.dot(a, b, preferred_element_type=F32)


def rms_scale(values, gain):
    mean_square = jnp.mean(values * values, axis=-1, keepdims=True)
    return (values * lax.rsqrt(mean_square + 1e-06) * gain).astype(BF16)


def kernel(
    sizes,
    queries_hbm,
    codes_hbm,
    ids_hbm,
    counts_hbm,
    centroids,
    buckets_hbm,
    candidates_hbm,
    input_proj_hbm,
    gain_one_hbm,
    query_proj,
    key_proj,
    value_proj,
    output_proj,
    gain_two_hbm,
    up_proj,
    down_proj,
    out,
    queries,
    q_own,
    ids,
    counts,
    buckets,
    candidates,
    input_proj,
    gain_one,
    gain_two,
    codes,
    cent_bf,
    table,
    embed,
    q_all,
    outbox,
    inbox,
    normed,
    hidden,
    wq,
    wk,
    wv,
    wo,
    wu,
    wd,
    load_sem,
    ids_sem,
    q_send,
    q_recv,
    b_send,
    b_recv,
):
    n_docs, n_cent, n_sub = sizes
    members = n_cent * n_sub
    total = n_docs * members
    docs_local = codes.shape[0]
    pad = codes.shape[1] * 2 // DIM
    tiles, pairs = docs_local // 8, pad // 2
    rows = docs_local // 4
    cand = candidates.shape[1]
    mine = cand // members

    z = lax.axis_index("docs")
    member = lax.axis_index("cent") * n_sub + lax.axis_index("sub")
    me = z * members + member

    def place(flat):
        return {
            "docs": shift(flat, members),
            "cent": shift(wrap(flat, members), n_sub),
            "sub": wrap(flat, n_sub),
        }

    def each(count, body):
        def step(i, carry):
            body(i)
            return carry

        lax.fori_loop(0, count, step, 0, unroll=count <= 16)

    parts = 4
    cent_rows = centroids.shape[0] // parts
    doc_rows = docs_local // parts
    cent_pieces = [
        (centroids.at[i * cent_rows : (i + 1) * cent_rows], cent_bf.at[i * cent_rows : (i + 1) * cent_rows])
        for i in range(parts)
    ]
    code_pieces = [
        (codes_hbm.at[0, i * doc_rows : (i + 1) * doc_rows], codes.at[i * doc_rows : (i + 1) * doc_rows])
        for i in range(parts)
    ]
    small = [(buckets_hbm, buckets), (counts_hbm, counts), (candidates_hbm, candidates)]
    late = [
        (input_proj_hbm, input_proj),
        (gain_one_hbm, gain_one),
        (gain_two_hbm, gain_two),
        (query_proj, wq),
        (key_proj, wk),
        (value_proj, wv),
        (output_proj, wo),
        (up_proj, wu),
        (down_proj, wd),
    ]
    order = [*small, (queries_hbm, queries), *cent_pieces, *code_pieces, *late]
    pulls = [
        pltpu.make_async_copy(src, dst, load_sem.at[i]) for i, (src, dst) in enumerate(order)
    ]
    query_pull = pulls[3]
    small_pulls, cent_pulls = pulls[0:3], pulls[4 : 4 + parts]
    code_pulls, late_pulls = pulls[4 + parts : 4 + 2 * parts], pulls[4 + 2 * parts :]
    apart = len(ids)
    for pull in pulls[: 4 + parts + 1]:
        pull.start()
    for s in range(apart):
        for t in range(docs_local // apart if apart > 1 else 0):
            pltpu.make_async_copy(
                ids_hbm.at[:, (t * apart + s) * pad : (t * apart + s + 1) * pad],
                ids[s].at[:, t * pad : (t + 1) * pad],
                ids_sem.at[s],
            ).start()
    if apart == 1:
        pltpu.make_async_copy(ids_hbm, ids[0], ids_sem.at[0]).start()
    for pull in code_pulls[1:]:
        pull.start()
    barrier = pltpu.get_barrier_semaphore()
    each(
        total - 1,
        lambda i: pl.semaphore_signal(barrier, inc=1, device_id=place(wrap(me + i + 1, total))),
    )
    for pull in small_pulls:
        pull.wait()

    live = column(counts[...])
    cand_col = column(candidates[...])
    low_levels, high_levels = buckets[0:8, :], buckets[8:16, :]
    lane = iota((8, DIM), 1)
    words = [(lane >> 1) + 64 * h for h in range(2)]
    nibble = (lane & 1) * 4

    def residual(word, h):
        code = lookup(word, words[h], 1) >> nibble
        level = code & 7
        return jnp.where(
            (code & 8) != 0,
            lookup(high_levels, level, 0),
            lookup(low_levels, level, 0),
        )

    def loop(first, last, body):
        def step(i, carry):
            body(i)
            return carry

        lax.fori_loop(first, last, step, 0)

    block = 256

    def widen(i):
        at = pl.ds(pl.multiple_of(i * block, block), block)
        table[at, :] = cent_bf[at, :].astype(F32)

    for i in range(parts):
        cent_pulls[i].wait()
        loop(i * cent_rows // block, (i + 1) * cent_rows // block, widen)
    sub = iota((8, DIM), 0)

    group = 16 if pairs % 16 == 0 else 2

    def tile(t):
        def pair(k):
            start = t * (8 // apart * pad) + k * (2 * group)
            for u in range(0, group, 2):
                at = pl.ds(pl.multiple_of(t * (pairs * 8) + k * (8 * group) + u * 8, 16), 16)
                both = [[], []]
                for v in range(u, u + 2):
                    word = codes[
                        pl.ds(pl.multiple_of(t * 8, 8), 8),
                        pl.ds(pl.multiple_of(k * (group * DIM) + v * DIM, DIM), DIM),
                    ]
                    for h in range(2):
                        acc = None
                        for s in range(8):
                            slot = ids[s % apart][0, start + (s % (8 // apart) * pad + 2 * v + h)]
                            row = jnp.broadcast_to(table[pl.ds(slot, 1), :], (8, DIM))
                            acc = row if acc is None else jnp.where(sub == s, row, acc)
                        both[h].append(acc + residual(word, h))
                for h in range(2):
                    embed[at, h * DIM : (h + 1) * DIM] = jnp.concatenate(both[h], axis=0).astype(BF16)

        loop(0, pairs // group, pair)

    def q_copy(i):
        to = wrap(member + i + 1, members)
        return pltpu.make_async_remote_copy(
            src_ref=q_own,
            dst_ref=q_all.at[member],
            send_sem=q_send.at[i],
            recv_sem=q_recv.at[member],
            device_id={"cent": shift(to, n_sub), "sub": wrap(to, n_sub)},
        )

    for s in range(apart):
        count = ids[s].shape[1]
        pltpu.make_async_copy(ids_hbm.at[:, 0:count], ids[s], ids_sem.at[s]).wait()
    query_pull.wait()
    q_own[...] = queries[...].astype(BF16)
    for i in range(parts):
        code_pulls[i].wait()
        loop(i * tiles // parts, (i + 1) * tiles // parts, tile)
        if i == 0:
            pl.semaphore_wait(barrier, total - 1)
            each(members - 1, lambda i: q_copy(i).start())
            for pull in late_pulls:
                pull.start()

    def q_wait(i):
        source = wrap(member + i + 1, members)
        pltpu.make_async_remote_copy(
            src_ref=q_own,
            dst_ref=q_all.at[source],
            send_sem=q_send.at[i],
            recv_sem=q_recv.at[source],
            device_id={"cent": shift(source, n_sub), "sub": wrap(source, n_sub)},
        ).wait()

    each(members - 1, q_wait)
    q_all[member] = q_own[...]
    q_rows = members * QT
    splits = q_rows // DIM
    zero = jnp.zeros((DIM, DIM), BF16)
    chunk = pairs
    for n in range(splits):
        q_bf = q_all[n * (DIM // QT) : (n + 1) * (DIM // QT)].reshape(DIM, DIM)
        weight = jnp.concatenate(
            [
                jnp.concatenate([q_bf, zero], axis=1),
                jnp.concatenate([zero, q_bf], axis=1),
            ],
            axis=0,
        )
        for t in range(tiles):
            live_t = jnp.broadcast_to(live[t * 8 : t * 8 + 8], (8, DIM))
            best = jnp.full((8, DIM), -1e30, F32)
            for k in range(0, pairs, chunk):
                at = (t * pairs + k) * 8
                scores = lax.dot_general(
                    embed[at : at + chunk * 8, :], weight, NT, preferred_element_type=F32
                )
                for u in range(chunk):
                    for h in range(2):
                        part = scores[u * 8 : u * 8 + 8, h * DIM : (h + 1) * DIM]
                        part = jnp.where(live_t > 2.0 * (k + u) + h, part, -1e30)
                        best = jnp.maximum(best, part)
            for g in range(4):
                to = t % 4
                moved = best if g == to else pltpu.roll(best, (to - g) * QT % DIM, 1)
                outbox[n * 4 + g, t // 4 * 8 : t // 4 * 8 + 8, to * QT : (to + 1) * QT] = moved[
                    :, to * QT : (to + 1) * QT
                ]

    def b_copy(i, flat, slot):
        return pltpu.make_async_remote_copy(
            src_ref=outbox.at[shift(flat, members)],
            dst_ref=inbox.at[slot],
            send_sem=b_send.at[i],
            recv_sem=b_recv.at[slot],
            device_id=place(flat),
        )

    def b_start(i):
        b_copy(i, i + jnp.where(i >= me, 1, 0), me).start()

    each(total - 1, b_start)
    inbox[me] = outbox[z]

    docs_all = n_docs * docs_local
    c_int = cand_col.astype(jnp.int32)
    within = c_int % docs_local
    row_of = c_int // docs_local * rows + within // 32 * 8 + within % 8
    lanes_of = within // 8 % 4
    one_hot = (iota((cand, docs_all // 4), 1) == row_of).astype(F32).astype(BF16)
    one_hot = jnp.concatenate([one_hot, one_hot], axis=1)
    for pull in late_pulls:
        pull.wait()
    in_high, in_low = halves(jnp.concatenate([input_proj[...]] * 4, axis=0))
    in_four = jnp.concatenate([in_high, in_high, in_low], axis=0)

    def b_wait(i):
        flat = wrap(me + i + 1, total)
        b_copy(i, flat, flat).wait()

    each(total - 1, b_wait)
    maxima = jnp.concatenate(
        [
            functools.reduce(jnp.maximum, [inbox[d * members + m] for m in range(members)])
            for d in range(n_docs)
        ],
        axis=0,
    )
    picked = mm(one_hot, jnp.concatenate(halves(maxima), axis=0))
    picked = jnp.where(iota((cand, DIM), 1) // QT == lanes_of, picked, 0.0)
    high, low = halves(picked)
    all_hidden = mm(jnp.concatenate([high, low, high], axis=1), in_four)
    all_normed = rms_scale(all_hidden, gain_one[...])
    hidden[...] = all_hidden
    normed[...] = all_normed.astype(F32)
    here = pl.ds(pl.multiple_of(member * mine, 8), mine)
    hidden_zero = hidden[here, :]
    q_heads = mm(normed[here, :].astype(BF16), wq[...]).astype(BF16)
    k_heads = mm(all_normed, wk[...]).astype(BF16)
    v_heads = mm(all_normed, wv[...]).astype(BF16)
    head_of = iota((mine, H), 1) // HEAD
    q_stack = jnp.concatenate(
        [jnp.where(head_of == h, q_heads.astype(F32), 0.0) for h in range(HEADS)], axis=0
    ).astype(BF16)
    att = lax.dot_general(q_stack, k_heads, NT, preferred_element_type=F32) * HEAD ** (-0.5)
    expon = jnp.exp(att - jnp.max(att, axis=-1, keepdims=True))
    mixed = mm(expon.astype(BF16), v_heads) / jnp.sum(expon, axis=-1, keepdims=True)
    attended = functools.reduce(
        jnp.add,
        [
            jnp.where(head_of == h, mixed[h * mine : (h + 1) * mine], 0.0)
            for h in range(HEADS)
        ],
    ).astype(BF16)
    hidden_one = hidden_zero + mm(attended, wo[...])
    normed_two = rms_scale(hidden_one, gain_two[...])
    inner = jax.nn.gelu(mm(normed_two, wu[...])).astype(BF16)
    out[0] = hidden_one + mm(inner, wd[...])


def on_device(sizes, *args):
    (queries, codes, ids, counts, centroids, buckets, candidates, input_proj, gain_one) = args[:9]
    (query_proj, key_proj, value_proj, output_proj, gain_two, up_proj, down_proj) = args[9:]
    n_docs, n_cent, n_sub = sizes
    members = n_cent * n_sub
    total = n_docs * members
    docs_local, width = codes.shape[1:]
    cand = candidates.shape[1]
    slots = docs_local * width * 2 // DIM
    apart = 8 if (width * 2 // DIM) % DIM == 0 else 1
    vmem = pl.BlockSpec(memory_space=pltpu.VMEM)
    hbm = pl.BlockSpec(memory_space=pl.ANY)
    weights = (query_proj, key_proj, value_proj, output_proj, up_proj, down_proj)
    return pl.pallas_call(
        functools.partial(kernel, sizes),
        out_shape=pltpu.VMEM((1, cand // members, H), F32),
        in_specs=[hbm] * 16,
        out_specs=vmem,
        scratch_shapes=[
            pltpu.VMEM(queries.shape, F32),
            pltpu.VMEM(queries.shape, BF16),
            [pltpu.SMEM((1, ids.shape[1] // apart), jnp.int32) for _ in range(apart)],
            pltpu.VMEM(counts.shape, jnp.int32),
            pltpu.VMEM(buckets.shape, F32),
            pltpu.VMEM(candidates.shape, jnp.int32),
            pltpu.VMEM(input_proj.shape, F32),
            pltpu.VMEM((1, H), F32),
            pltpu.VMEM((1, H), F32),
            pltpu.VMEM((docs_local, width), jnp.int32),
            pltpu.VMEM(centroids.shape, BF16),
            pltpu.VMEM(centroids.shape, F32),
            pltpu.VMEM((slots // 2, 2 * DIM), BF16),
            pltpu.VMEM((members, QT, DIM), BF16),
            pltpu.VMEM((n_docs, docs_local // 4, DIM), F32),
            pltpu.VMEM((total, docs_local // 4, DIM), F32),
            pltpu.VMEM((cand, H), F32),
            pltpu.VMEM((cand, H), F32),
            *[pltpu.VMEM(w.shape, BF16) for w in weights],
            pltpu.SemaphoreType.DMA((22,)),
            pltpu.SemaphoreType.DMA((8,)),
            pltpu.SemaphoreType.DMA((members,)),
            pltpu.SemaphoreType.DMA((members,)),
            pltpu.SemaphoreType.DMA((total,)),
            pltpu.SemaphoreType.DMA((total,)),
        ],
        compiler_params=pltpu.CompilerParams(collective_id=0, has_side_effects=True),
    )(
        queries,
        codes,
        ids,
        counts,
        centroids,
        buckets,
        candidates,
        input_proj,
        gain_one.reshape(1, H),
        query_proj,
        key_proj,
        value_proj,
        output_proj,
        gain_two.reshape(1, H),
        up_proj,
        down_proj,
    )


def solution(mesh):
    in_specs = (
        P(("groups", "cent", "sub"), None),
        P(("cent", "sub"), ("groups", "docs"), None),
        P(("cent", "sub"), ("groups", "docs")),
        P(("cent", "sub"), ("groups", "docs")),
        P(("cent", "sub"), None),
        P(),
        P(("groups", "docs"), None),
        P(),
        P(),
        P(),
        P(),
        P(),
        P(),
        P(),
        P(),
        P(),
    )
    out_specs = P(("groups", "docs"), ("cent", "sub"), None)
    sizes = tuple(mesh.shape[name] for name in AXES)
    return jax.shard_map(
        functools.partial(on_device, sizes),
        mesh=mesh,
        in_specs=in_specs,
        out_specs=out_specs,
        check_vma=False,
    )
```

```python
import functools

import jax
import jax.numpy as jnp
from jax import lax
from jax.experimental import pallas as pl
from jax.experimental.pallas import tpu as pltpu
from jax.sharding import PartitionSpec as P

DIM = 128
QT = 32
H = 256
HEADS = 4
HEAD = 64
F32 = jnp.float32
BF16 = jnp.bfloat16
NT = (((1,), (1,)), ((), ()))
AXES = ("docs", "cent", "sub")


def iota(shape, axis):
    return lax.broadcasted_iota(jnp.int32, shape, axis)


def column(row):
    n = row.shape[1]
    wide = jnp.broadcast_to(row.astype(F32), (n, n))
    return jnp.sum(jnp.where(iota((n, n), 0) == iota((n, n), 1), wide, 0.0), axis=1, keepdims=True)


def wrap(value, size):
    return value & (size - 1) if size & (size - 1) == 0 else lax.rem(value, size)


def shift(value, size):
    return value >> (size.bit_length() - 1) if size & (size - 1) == 0 else lax.div(value, size)


def lookup(table, index, axis):
    numbers = lax.GatherDimensionNumbers(
        offset_dims=(),
        collapsed_slice_dims=(axis,),
        start_index_map=(axis,),
        operand_batching_dims=(1 - axis,),
        start_indices_batching_dims=(1 - axis,),
    )
    return lax.gather(
        table,
        index[..., None],
        numbers,
        slice_sizes=(1, 1),
        mode=lax.GatherScatterMode.PROMISE_IN_BOUNDS,
    )


def halves(values):
    high = values.astype(BF16)
    return high, (values - high.astype(F32)).astype(BF16)


def mm(a, b):
    return jnp.dot(a, b, preferred_element_type=F32)


def rms(values):
    return lax.rsqrt(jnp.mean(values * values, axis=-1, keepdims=True) + 1e-06)


def kernel(
    sizes,
    queries_hbm,
    codes_hbm,
    ids_hbm,
    counts_hbm,
    centroids,
    buckets_hbm,
    candidates_hbm,
    input_proj_hbm,
    gain_one_hbm,
    query_proj,
    key_proj,
    value_proj,
    output_proj,
    gain_two_hbm,
    up_proj,
    down_proj,
    out,
    queries,
    q_own,
    ids,
    counts,
    buckets,
    candidates,
    input_proj,
    gain_one,
    gain_two,
    codes,
    cent_bf,
    table,
    embed,
    q_all,
    outbox,
    inbox,
    hidden,
    wq,
    wk,
    wv,
    wo,
    wu,
    wd,
    load_sem,
    ids_sem,
    q_sem,
    b_sem,
):
    n_docs, n_cent, n_sub = sizes
    members = n_cent * n_sub
    total = n_docs * members
    docs_local = codes.shape[0]
    pad = codes.shape[1] * 2 // DIM
    tiles, pairs = docs_local // 8, pad // 2
    rows = docs_local // 4
    cand = candidates.shape[1]
    mine = cand // members

    z = lax.axis_index("docs")
    member = lax.axis_index("cent") * n_sub + lax.axis_index("sub")
    me = z * members + member

    def place(flat):
        return {
            "docs": shift(flat, members),
            "cent": shift(wrap(flat, members), n_sub),
            "sub": wrap(flat, n_sub),
        }

    def each(count, body):
        def step(i, carry):
            body(i)
            return carry

        lax.fori_loop(0, count, step, 0, unroll=count <= 16)

    parts = 4
    cent_rows = centroids.shape[0] // parts
    doc_rows = docs_local // parts
    cent_pieces = [
        (centroids.at[i * cent_rows : (i + 1) * cent_rows], cent_bf.at[i * cent_rows : (i + 1) * cent_rows])
        for i in range(parts)
    ]
    code_pieces = [
        (codes_hbm.at[0, i * doc_rows : (i + 1) * doc_rows], codes.at[i * doc_rows : (i + 1) * doc_rows])
        for i in range(parts)
    ]
    small = [(buckets_hbm, buckets), (counts_hbm, counts), (candidates_hbm, candidates)]
    late = [
        (input_proj_hbm, input_proj),
        (gain_one_hbm, gain_one),
        (gain_two_hbm, gain_two),
        (query_proj, wq),
        (key_proj, wk),
        (value_proj, wv),
        (output_proj, wo),
        (up_proj, wu),
        (down_proj, wd),
    ]
    order = [*small, (queries_hbm, queries), *cent_pieces, *code_pieces, *late]
    first = 4 + 2 * parts
    pulls = [
        pltpu.make_async_copy(src, dst, load_sem.at[i % first]) for i, (src, dst) in enumerate(order)
    ]
    query_pull = pulls[3]
    small_pulls, cent_pulls = pulls[0:3], pulls[4 : 4 + parts]
    code_pulls, late_pulls = pulls[4 + parts : 4 + 2 * parts], pulls[4 + 2 * parts :]
    apart = len(ids)
    for pull in pulls[: 4 + parts + 1]:
        pull.start()
    for s in range(apart):
        for t in range(docs_local // apart if apart > 1 else 0):
            pltpu.make_async_copy(
                ids_hbm.at[:, (t * apart + s) * pad : (t * apart + s + 1) * pad],
                ids[s].at[:, t * pad : (t + 1) * pad],
                ids_sem.at[0],
            ).start()
    if apart == 1:
        pltpu.make_async_copy(ids_hbm, ids[0], ids_sem.at[0]).start()
    for pull in code_pulls[1:]:
        pull.start()
    barrier = pltpu.get_barrier_semaphore()
    each(
        total - 1,
        lambda i: pl.semaphore_signal(barrier, inc=1, device_id=place(wrap(me + i + 1, total))),
    )
    for pull in small_pulls:
        pull.wait()

    live = column(counts[...])
    cand_col = column(candidates[...])
    low_levels, high_levels = buckets[0:8, :], buckets[8:16, :]
    lane = iota((8, DIM), 1)
    words = [(lane >> 1) + 64 * h for h in range(2)]
    nibble = (lane & 1) * 4

    def residual(word, h):
        code = lookup(word, words[h], 1) >> nibble
        level = code & 7
        return jnp.where(
            (code & 8) != 0,
            lookup(high_levels, level, 0),
            lookup(low_levels, level, 0),
        )

    def loop(first, last, body):
        def step(i, carry):
            body(i)
            return carry

        lax.fori_loop(first, last, step, 0)

    block = 256

    def widen(i):
        at = pl.ds(pl.multiple_of(i * block, block), block)
        table[at, :] = cent_bf[at, :].astype(F32)

    for i in range(parts):
        cent_pulls[i].wait()
        loop(i * cent_rows // block, (i + 1) * cent_rows // block, widen)
    sub = iota((8, DIM), 0)

    group = 16 if pairs % 16 == 0 else 2

    steps = pairs // group

    def rebuild(i):
        t, k = shift(i, steps), wrap(i, steps)
        start = t * (8 // apart * pad) + k * (2 * group)
        for u in range(0, group, 2):
            at = pl.ds(pl.multiple_of(t * (pairs * 8) + k * (8 * group) + u * 8, 16), 16)
            both = [[], []]
            for v in range(u, u + 2):
                word = codes[
                    pl.ds(pl.multiple_of(t * 8, 8), 8),
                    pl.ds(pl.multiple_of(k * (group * DIM) + v * DIM, DIM), DIM),
                ]
                for h in range(2):
                    acc = None
                    for s in range(8):
                        slot = ids[s % apart][0, start + (s % (8 // apart) * pad + 2 * v + h)]
                        row = jnp.broadcast_to(table[pl.ds(slot, 1), :], (8, DIM))
                        acc = row if acc is None else jnp.where(sub == s, row, acc)
                    both[h].append(acc + residual(word, h))
            for h in range(2):
                embed[at, h * DIM : (h + 1) * DIM] = jnp.concatenate(both[h], axis=0).astype(BF16)

    def q_copy(i):
        to = wrap(member + i + 1, members)
        return pltpu.make_async_remote_copy(
            src_ref=q_own,
            dst_ref=q_all.at[member],
            send_sem=q_sem.at[0],
            recv_sem=q_sem.at[1],
            device_id={"cent": shift(to, n_sub), "sub": wrap(to, n_sub)},
        )

    pltpu.make_async_copy(ids_hbm, ids_hbm, ids_sem.at[0]).wait()
    query_pull.wait()
    q_own[...] = queries[...].astype(BF16)
    for i in range(parts):
        code_pulls[i].wait()
        begin, end = (j * tiles * steps // parts for j in (i, i + 1))
        if i == 0:
            loop(begin, begin + 2, rebuild)
            begin += 2
            pl.semaphore_wait(barrier, total - 1)
            each(members - 1, lambda i: q_copy(i).start())
        loop(begin, end, rebuild)
        if i == 0:
            for pull in late_pulls:
                pull.start()

    for i in range(2):
        others = q_all.at[0 : members - 1]
        pltpu.make_async_copy(others, others, q_sem.at[i]).wait()
    q_all[member] = q_own[...]
    q_rows = members * QT
    splits = q_rows // DIM
    zero = jnp.zeros((DIM, DIM), BF16)
    chunk = pairs
    for n in range(splits):
        q_bf = q_all[n * (DIM // QT) : (n + 1) * (DIM // QT)].reshape(DIM, DIM)
        weight = jnp.concatenate(
            [
                jnp.concatenate([q_bf, zero], axis=1),
                jnp.concatenate([zero, q_bf], axis=1),
            ],
            axis=0,
        )
        for t in range(tiles):
            live_t = jnp.broadcast_to(live[t * 8 : t * 8 + 8], (8, DIM))
            best = jnp.full((8, DIM), -1e30, F32)
            for k in range(0, pairs, chunk):
                at = (t * pairs + k) * 8
                scores = lax.dot_general(
                    embed[at : at + chunk * 8, :], weight, NT, preferred_element_type=F32
                )
                for u in range(chunk):
                    for h in range(2):
                        part = scores[u * 8 : u * 8 + 8, h * DIM : (h + 1) * DIM]
                        part = jnp.where(live_t > 2.0 * (k + u) + h, part, -1e30)
                        best = jnp.maximum(best, part)
            for g in range(4):
                to = t % 4
                moved = best if g == to else pltpu.roll(best, (to - g) * QT % DIM, 1)
                outbox[n * 4 + g, t // 4 * 8 : t // 4 * 8 + 8, to * QT : (to + 1) * QT] = moved[
                    :, to * QT : (to + 1) * QT
                ]

    def b_copy(flat, slot):
        return pltpu.make_async_remote_copy(
            src_ref=outbox.at[shift(flat, members)],
            dst_ref=inbox.at[slot],
            send_sem=b_sem.at[0],
            recv_sem=b_sem.at[1],
            device_id=place(flat),
        )

    def b_start(i):
        b_copy(i + jnp.where(i >= me, 1, 0), me).start()

    each(total - 1, b_start)
    inbox[me] = outbox[z]

    docs_all = n_docs * docs_local
    c_int = cand_col.astype(jnp.int32)
    within = c_int % docs_local
    row_of = c_int // docs_local * rows + within // 32 * 8 + within % 8
    lanes_of = within // 8 % 4
    one_hot = (iota((cand, docs_all // 4), 1) == row_of).astype(F32).astype(BF16)
    one_hot = jnp.concatenate([one_hot, one_hot], axis=1)
    for pull in late_pulls:
        pull.wait()
    in_high, in_low = halves(jnp.concatenate([input_proj[...]] * 4, axis=0))
    in_four = jnp.concatenate([in_high, in_high, in_low], axis=0)

    for i in range(2):
        others = inbox.at[0 : total - 1]
        pltpu.make_async_copy(others, others, b_sem.at[i]).wait()
    maxima = jnp.concatenate(
        [
            functools.reduce(jnp.maximum, [inbox[d * members + m] for m in range(members)])
            for d in range(n_docs)
        ],
        axis=0,
    )
    picked = mm(one_hot, jnp.concatenate(halves(maxima), axis=0))
    picked = jnp.where(iota((cand, DIM), 1) // QT == lanes_of, picked, 0.0)
    high, low = halves(picked)
    all_hidden = mm(jnp.concatenate([high, low, high], axis=1), in_four)
    all_scale = rms(all_hidden)
    all_gained = (all_hidden * gain_one[...]).astype(BF16)
    hidden[...] = all_hidden
    here = pl.ds(pl.multiple_of(member * mine, 8), mine)
    hidden_zero = hidden[here, :]
    gained = (hidden_zero * gain_one[...]).astype(BF16)
    k_heads = (mm(all_gained, wk[...]) * all_scale).astype(BF16)
    q_heads = (mm(gained, wq[...]) * rms(hidden_zero)).astype(BF16)
    v_heads = (mm(all_gained, wv[...]) * all_scale).astype(BF16)
    head_of = iota((mine, H), 1) // HEAD
    q_stack = jnp.concatenate(
        [jnp.where(head_of == h, q_heads.astype(F32), 0.0) for h in range(HEADS)], axis=0
    ).astype(BF16)
    att = lax.dot_general(q_stack, k_heads, NT, preferred_element_type=F32) * HEAD ** (-0.5)
    expon = jnp.exp(att - jnp.max(att, axis=-1, keepdims=True))
    mixed = mm(expon.astype(BF16), v_heads) / jnp.sum(expon, axis=-1, keepdims=True)
    attended = functools.reduce(
        jnp.add,
        [
            jnp.where(head_of == h, mixed[h * mine : (h + 1) * mine], 0.0)
            for h in range(HEADS)
        ],
    ).astype(BF16)
    hidden_one = hidden_zero + mm(attended, wo[...])
    gained_two = (hidden_one * gain_two[...]).astype(BF16)
    inner = jax.nn.gelu(mm(gained_two, wu[...]) * rms(hidden_one)).astype(BF16)
    out[0] = hidden_one + mm(inner, wd[...])


def on_device(sizes, *args):
    (queries, codes, ids, counts, centroids, buckets, candidates, input_proj, gain_one) = args[:9]
    (query_proj, key_proj, value_proj, output_proj, gain_two, up_proj, down_proj) = args[9:]
    n_docs, n_cent, n_sub = sizes
    members = n_cent * n_sub
    total = n_docs * members
    docs_local, width = codes.shape[1:]
    cand = candidates.shape[1]
    slots = docs_local * width * 2 // DIM
    apart = 8 if (width * 2 // DIM) % DIM == 0 else 1
    vmem = pl.BlockSpec(memory_space=pltpu.VMEM)
    hbm = pl.BlockSpec(memory_space=pl.ANY)
    weights = (query_proj, key_proj, value_proj, output_proj, up_proj, down_proj)
    return pl.pallas_call(
        functools.partial(kernel, sizes),
        out_shape=pltpu.VMEM((1, cand // members, H), F32),
        in_specs=[hbm] * 16,
        out_specs=vmem,
        scratch_shapes=[
            pltpu.VMEM(queries.shape, F32),
            pltpu.VMEM(queries.shape, BF16),
            [pltpu.SMEM((1, ids.shape[1] // apart), jnp.int32) for _ in range(apart)],
            pltpu.VMEM(counts.shape, jnp.int32),
            pltpu.VMEM(buckets.shape, F32),
            pltpu.VMEM(candidates.shape, jnp.int32),
            pltpu.VMEM(input_proj.shape, F32),
            pltpu.VMEM((1, H), F32),
            pltpu.VMEM((1, H), F32),
            pltpu.VMEM((docs_local, width), jnp.int32),
            pltpu.VMEM(centroids.shape, BF16),
            pltpu.VMEM(centroids.shape, F32),
            pltpu.VMEM((slots // 2, 2 * DIM), BF16),
            pltpu.VMEM((members, QT, DIM), BF16),
            pltpu.VMEM((n_docs, docs_local // 4, DIM), F32),
            pltpu.VMEM((total, docs_local // 4, DIM), F32),
            pltpu.VMEM((cand, H), F32),
            *[pltpu.VMEM(w.shape, BF16) for w in weights],
            pltpu.SemaphoreType.DMA((12,)),
            pltpu.SemaphoreType.DMA((1,)),
            pltpu.SemaphoreType.DMA((2,)),
            pltpu.SemaphoreType.DMA((2,)),
        ],
        compiler_params=pltpu.CompilerParams(collective_id=0, has_side_effects=True),
    )(
        queries,
        codes,
        ids,
        counts,
        centroids,
        buckets,
        candidates,
        input_proj,
        gain_one.reshape(1, H),
        query_proj,
        key_proj,
        value_proj,
        output_proj,
        gain_two.reshape(1, H),
        up_proj,
        down_proj,
    )


def solution(mesh):
    in_specs = (
        P(("groups", "cent", "sub"), None),
        P(("cent", "sub"), ("groups", "docs"), None),
        P(("cent", "sub"), ("groups", "docs")),
        P(("cent", "sub"), ("groups", "docs")),
        P(("cent", "sub"), None),
        P(),
        P(("groups", "docs"), None),
        P(),
        P(),
        P(),
        P(),
        P(),
        P(),
        P(),
        P(),
        P(),
    )
    out_specs = P(("groups", "docs"), ("cent", "sub"), None)
    sizes = tuple(mesh.shape[name] for name in AXES)
    return jax.shard_map(
        functools.partial(on_device, sizes),
        mesh=mesh,
        in_specs=in_specs,
        out_specs=out_specs,
        check_vma=False,
    )
```

```python
import functools

import jax
import jax.numpy as jnp
from jax import lax
from jax.experimental import pallas as pl
from jax.experimental.pallas import tpu as pltpu
from jax.sharding import PartitionSpec as P

DIM = 128
QT = 32
H = 256
HEADS = 4
HEAD = 64
F32 = jnp.float32
BF16 = jnp.bfloat16
NT = (((1,), (1,)), ((), ()))
AXES = ("docs", "cent", "sub")


def iota(shape, axis):
    return lax.broadcasted_iota(jnp.int32, shape, axis)


def column(row):
    n = row.shape[1]
    wide = jnp.broadcast_to(row.astype(F32), (n, n))
    return jnp.sum(jnp.where(iota((n, n), 0) == iota((n, n), 1), wide, 0.0), axis=1, keepdims=True)


def wrap(value, size):
    return value & (size - 1) if size & (size - 1) == 0 else lax.rem(value, size)


def shift(value, size):
    return value >> (size.bit_length() - 1) if size & (size - 1) == 0 else lax.div(value, size)


def lookup(table, index, axis):
    numbers = lax.GatherDimensionNumbers(
        offset_dims=(),
        collapsed_slice_dims=(axis,),
        start_index_map=(axis,),
        operand_batching_dims=(1 - axis,),
        start_indices_batching_dims=(1 - axis,),
    )
    return lax.gather(
        table,
        index[..., None],
        numbers,
        slice_sizes=(1, 1),
        mode=lax.GatherScatterMode.PROMISE_IN_BOUNDS,
    )


def halves(values):
    high = values.astype(BF16)
    return high, (values - high.astype(F32)).astype(BF16)


def mm(a, b):
    return jnp.dot(a, b, preferred_element_type=F32)


def rms(values):
    return lax.rsqrt(jnp.mean(values * values, axis=-1, keepdims=True) + 1e-06)


def kernel(
    sizes,
    queries_hbm,
    codes_hbm,
    ids_hbm,
    counts_hbm,
    centroids,
    buckets_hbm,
    candidates_hbm,
    input_proj_hbm,
    gain_one_hbm,
    query_proj,
    key_proj,
    value_proj,
    output_proj,
    gain_two_hbm,
    up_proj,
    down_proj,
    out,
    queries,
    q_own,
    ids,
    counts,
    buckets,
    candidates,
    input_proj,
    gain_one,
    gain_two,
    codes,
    cent_bf,
    table,
    embed,
    q_all,
    outbox,
    inbox,
    hidden,
    wq,
    wk,
    wv,
    wo,
    wu,
    wd,
    load_sem,
    ids_sem,
    q_sem,
    b_sem,
):
    n_docs, n_cent, n_sub = sizes
    members = n_cent * n_sub
    total = n_docs * members
    docs_local = codes.shape[0]
    pad = codes.shape[1] * 2 // DIM
    tiles, pairs = docs_local // 8, pad // 2
    rows = docs_local // 4
    cand = candidates.shape[1]
    mine = cand // members

    z = lax.axis_index("docs")
    member = lax.axis_index("cent") * n_sub + lax.axis_index("sub")
    me = z * members + member

    def place(flat):
        return {
            "docs": shift(flat, members),
            "cent": shift(wrap(flat, members), n_sub),
            "sub": wrap(flat, n_sub),
        }

    def each(count, body):
        def step(i, carry):
            body(i)
            return carry

        lax.fori_loop(0, count, step, 0, unroll=count <= 16)

    parts = 4
    cent_rows = centroids.shape[0] // parts
    doc_rows = docs_local // parts
    cent_pieces = [
        (centroids.at[i * cent_rows : (i + 1) * cent_rows], cent_bf.at[i * cent_rows : (i + 1) * cent_rows])
        for i in range(parts)
    ]
    code_pieces = [
        (codes_hbm.at[0, i * doc_rows : (i + 1) * doc_rows], codes.at[i * doc_rows : (i + 1) * doc_rows])
        for i in range(parts)
    ]
    small = [(buckets_hbm, buckets), (counts_hbm, counts), (candidates_hbm, candidates)]
    late = [
        (input_proj_hbm, input_proj),
        (gain_one_hbm, gain_one),
        (gain_two_hbm, gain_two),
        (query_proj, wq),
        (key_proj, wk),
        (value_proj, wv),
        (output_proj, wo),
        (up_proj, wu),
        (down_proj, wd),
    ]
    order = [*small, (queries_hbm, queries), *cent_pieces, *code_pieces, *late]
    first = 4 + 2 * parts
    pulls = [
        pltpu.make_async_copy(src, dst, load_sem.at[i % first]) for i, (src, dst) in enumerate(order)
    ]
    query_pull = pulls[3]
    small_pulls, cent_pulls = pulls[0:3], pulls[4 : 4 + parts]
    code_pulls, late_pulls = pulls[4 + parts : 4 + 2 * parts], pulls[4 + 2 * parts :]
    apart = len(ids)
    for pull in (*small_pulls, *cent_pulls):
        pull.start()
    barrier = pltpu.get_barrier_semaphore()
    each(
        total - 1,
        lambda i: pl.semaphore_signal(barrier, inc=1, device_id=place(wrap(me + i + 1, total))),
    )
    for pull in (code_pulls[0], query_pull):
        pull.start()
    for s in range(apart):
        for t in range(docs_local // apart if apart > 1 else 0):
            pltpu.make_async_copy(
                ids_hbm.at[:, (t * apart + s) * pad : (t * apart + s + 1) * pad],
                ids[s].at[:, t * pad : (t + 1) * pad],
                ids_sem.at[0],
            ).start()
    if apart == 1:
        pltpu.make_async_copy(ids_hbm, ids[0], ids_sem.at[0]).start()
    for pull in code_pulls[1:]:
        pull.start()
    for pull in small_pulls:
        pull.wait()

    live = column(counts[...])
    cand_col = column(candidates[...])
    low_levels, high_levels = buckets[0:8, :], buckets[8:16, :]
    lane = iota((8, DIM), 1)
    words = [(lane >> 1) + 64 * h for h in range(2)]
    nibble = (lane & 1) * 4

    def residual(word, h):
        code = lookup(word, words[h], 1) >> nibble
        level = code & 7
        return jnp.where(
            (code & 8) != 0,
            lookup(high_levels, level, 0),
            lookup(low_levels, level, 0),
        )

    def loop(first, last, body):
        def step(i, carry):
            body(i)
            return carry

        lax.fori_loop(first, last, step, 0)

    block = 256

    def widen(i):
        at = pl.ds(pl.multiple_of(i * block, block), block)
        table[at, :] = cent_bf[at, :].astype(F32)

    for i in range(parts):
        cent_pulls[i].wait()
        loop(i * cent_rows // block, (i + 1) * cent_rows // block, widen)
    sub = iota((8, DIM), 0)

    group = 16 if pairs % 16 == 0 else 2

    steps = pairs // group

    def rebuild(i):
        t, k = shift(i, steps), wrap(i, steps)
        start = t * (8 // apart * pad) + k * (2 * group)
        near_codes = codes.at[
            pl.ds(pl.multiple_of(t * 8, 8), 8),
            pl.ds(pl.multiple_of(k * (group * DIM), group * DIM), group * DIM),
        ]
        near_embed = embed.at[pl.ds(pl.multiple_of(i * (group * 8), group * 8), group * 8)]
        for u in range(0, group, 2):
            at = slice(u * 8, u * 8 + 16)
            both = [[], []]
            for v in range(u, u + 2):
                word = near_codes[:, v * DIM : (v + 1) * DIM]
                for h in range(2):
                    acc = None
                    for s in range(8):
                        slot = ids[s % apart][0, start + (s % (8 // apart) * pad + 2 * v + h)]
                        row = jnp.broadcast_to(table[pl.ds(slot, 1), :], (8, DIM))
                        acc = row if acc is None else jnp.where(sub == s, row, acc)
                    both[h].append(acc + residual(word, h))
            for h in range(2):
                near_embed[at, h * DIM : (h + 1) * DIM] = jnp.concatenate(both[h], axis=0).astype(BF16)

    def q_copy(i):
        to = wrap(member + i + 1, members)
        return pltpu.make_async_remote_copy(
            src_ref=q_own,
            dst_ref=q_all.at[member],
            send_sem=q_sem.at[0],
            recv_sem=q_sem.at[1],
            device_id={"cent": shift(to, n_sub), "sub": wrap(to, n_sub)},
        )

    pltpu.make_async_copy(ids_hbm, ids_hbm, ids_sem.at[0]).wait()
    query_pull.wait()
    q_own[...] = queries[...].astype(BF16)
    for i in range(parts):
        code_pulls[i].wait()
        begin, end = (j * tiles * steps // parts for j in (i, i + 1))
        if i == 0:
            loop(begin, begin + 0, rebuild)
            begin += 0
            pl.semaphore_wait(barrier, total - 1)
            each(members - 1, lambda i: q_copy(i).start())
        loop(begin, end, rebuild)
        if i == 0:
            for pull in late_pulls:
                pull.start()

    for i in range(2):
        others = q_all.at[0 : members - 1]
        pltpu.make_async_copy(others, others, q_sem.at[i]).wait()
    q_all[member] = q_own[...]
    q_rows = members * QT
    splits = q_rows // DIM
    zero = jnp.zeros((DIM, DIM), BF16)
    chunk = pairs
    for n in range(splits):
        q_bf = q_all[n * (DIM // QT) : (n + 1) * (DIM // QT)].reshape(DIM, DIM)
        weight = jnp.concatenate(
            [
                jnp.concatenate([q_bf, zero], axis=1),
                jnp.concatenate([zero, q_bf], axis=1),
            ],
            axis=0,
        )
        for t in range(tiles):
            live_t = jnp.broadcast_to(live[t * 8 : t * 8 + 8], (8, DIM))
            best = jnp.full((8, DIM), -1e30, F32)
            for k in range(0, pairs, chunk):
                at = (t * pairs + k) * 8
                scores = lax.dot_general(
                    embed[at : at + chunk * 8, :], weight, NT, preferred_element_type=F32
                )
                for u in range(chunk):
                    for h in range(2):
                        part = scores[u * 8 : u * 8 + 8, h * DIM : (h + 1) * DIM]
                        part = jnp.where(live_t > 2.0 * (k + u) + h, part, -1e30)
                        best = jnp.maximum(best, part)
            for g in range(4):
                to = t % 4
                moved = best if g == to else pltpu.roll(best, (to - g) * QT % DIM, 1)
                outbox[n * 4 + g, t // 4 * 8 : t // 4 * 8 + 8, to * QT : (to + 1) * QT] = moved[
                    :, to * QT : (to + 1) * QT
                ]

    def b_copy(flat, slot):
        return pltpu.make_async_remote_copy(
            src_ref=outbox.at[shift(flat, members)],
            dst_ref=inbox.at[slot],
            send_sem=b_sem.at[0],
            recv_sem=b_sem.at[1],
            device_id=place(flat),
        )

    def b_start(i):
        b_copy(i + jnp.where(i >= me, 1, 0), me).start()

    each(total - 1, b_start)
    inbox[me] = outbox[z]

    docs_all = n_docs * docs_local
    c_int = cand_col.astype(jnp.int32)
    within = c_int % docs_local
    row_of = c_int // docs_local * rows + within // 32 * 8 + within % 8
    lanes_of = within // 8 % 4
    one_hot = (iota((cand, docs_all // 4), 1) == row_of).astype(F32).astype(BF16)
    one_hot = jnp.concatenate([one_hot, one_hot], axis=1)
    for pull in late_pulls:
        pull.wait()
    in_high, in_low = halves(jnp.concatenate([input_proj[...]] * 4, axis=0))
    in_four = jnp.concatenate([in_high, in_high, in_low], axis=0)

    for i in range(2):
        others = inbox.at[0 : total - 1]
        pltpu.make_async_copy(others, others, b_sem.at[i]).wait()
    maxima = jnp.concatenate(
        [
            functools.reduce(jnp.maximum, [inbox[d * members + m] for m in range(members)])
            for d in range(n_docs)
        ],
        axis=0,
    )
    picked = mm(one_hot, jnp.concatenate(halves(maxima), axis=0))
    picked = jnp.where(iota((cand, DIM), 1) // QT == lanes_of, picked, 0.0)
    high, low = halves(picked)
    all_hidden = mm(jnp.concatenate([high, low, high], axis=1), in_four)
    all_scale = rms(all_hidden)
    all_gained = (all_hidden * gain_one[...]).astype(BF16)
    hidden[...] = all_hidden
    here = pl.ds(pl.multiple_of(member * mine, 8), mine)
    hidden_zero = hidden[here, :]
    gained = (hidden_zero * gain_one[...]).astype(BF16)
    k_heads = (mm(all_gained, wk[...]) * all_scale).astype(BF16)
    q_heads = (mm(gained, wq[...]) * rms(hidden_zero)).astype(BF16)
    v_heads = (mm(all_gained, wv[...]) * all_scale).astype(BF16)
    head_of = iota((mine, H), 1) // HEAD
    q_stack = jnp.concatenate(
        [jnp.where(head_of == h, q_heads.astype(F32), 0.0) for h in range(HEADS)], axis=0
    ).astype(BF16)
    att = lax.dot_general(q_stack, k_heads, NT, preferred_element_type=F32) * HEAD ** (-0.5)
    expon = jnp.exp(att - jnp.max(att, axis=-1, keepdims=True))
    mixed = mm(expon.astype(BF16), v_heads) / jnp.sum(expon, axis=-1, keepdims=True)
    attended = functools.reduce(
        jnp.add,
        [
            jnp.where(head_of == h, mixed[h * mine : (h + 1) * mine], 0.0)
            for h in range(HEADS)
        ],
    ).astype(BF16)
    hidden_one = hidden_zero + mm(attended, wo[...])
    gained_two = (hidden_one * gain_two[...]).astype(BF16)
    inner = jax.nn.gelu(mm(gained_two, wu[...]) * rms(hidden_one)).astype(BF16)
    out[0] = hidden_one + mm(inner, wd[...])


def on_device(sizes, *args):
    (queries, codes, ids, counts, centroids, buckets, candidates, input_proj, gain_one) = args[:9]
    (query_proj, key_proj, value_proj, output_proj, gain_two, up_proj, down_proj) = args[9:]
    n_docs, n_cent, n_sub = sizes
    members = n_cent * n_sub
    total = n_docs * members
    docs_local, width = codes.shape[1:]
    cand = candidates.shape[1]
    slots = docs_local * width * 2 // DIM
    apart = 8 if (width * 2 // DIM) % DIM == 0 else 1
    vmem = pl.BlockSpec(memory_space=pltpu.VMEM)
    hbm = pl.BlockSpec(memory_space=pl.ANY)
    weights = (query_proj, key_proj, value_proj, output_proj, up_proj, down_proj)
    return pl.pallas_call(
        functools.partial(kernel, sizes),
        out_shape=pltpu.VMEM((1, cand // members, H), F32),
        in_specs=[hbm] * 16,
        out_specs=vmem,
        scratch_shapes=[
            pltpu.VMEM(queries.shape, F32),
            pltpu.VMEM(queries.shape, BF16),
            [pltpu.SMEM((1, ids.shape[1] // apart), jnp.int32) for _ in range(apart)],
            pltpu.VMEM(counts.shape, jnp.int32),
            pltpu.VMEM(buckets.shape, F32),
            pltpu.VMEM(candidates.shape, jnp.int32),
            pltpu.VMEM(input_proj.shape, F32),
            pltpu.VMEM((1, H), F32),
            pltpu.VMEM((1, H), F32),
            pltpu.VMEM((docs_local, width), jnp.int32),
            pltpu.VMEM(centroids.shape, BF16),
            pltpu.VMEM(centroids.shape, F32),
            pltpu.VMEM((slots // 2, 2 * DIM), BF16),
            pltpu.VMEM((members, QT, DIM), BF16),
            pltpu.VMEM((n_docs, docs_local // 4, DIM), F32),
            pltpu.VMEM((total, docs_local // 4, DIM), F32),
            pltpu.VMEM((cand, H), F32),
            *[pltpu.VMEM(w.shape, BF16) for w in weights],
            pltpu.SemaphoreType.DMA((12,)),
            pltpu.SemaphoreType.DMA((1,)),
            pltpu.SemaphoreType.DMA((2,)),
            pltpu.SemaphoreType.DMA((2,)),
        ],
        compiler_params=pltpu.CompilerParams(collective_id=0, has_side_effects=True),
    )(
        queries,
        codes,
        ids,
        counts,
        centroids,
        buckets,
        candidates,
        input_proj,
        gain_one.reshape(1, H),
        query_proj,
        key_proj,
        value_proj,
        output_proj,
        gain_two.reshape(1, H),
        up_proj,
        down_proj,
    )


def solution(mesh):
    in_specs = (
        P(("groups", "cent", "sub"), None),
        P(("cent", "sub"), ("groups", "docs"), None),
        P(("cent", "sub"), ("groups", "docs")),
        P(("cent", "sub"), ("groups", "docs")),
        P(("cent", "sub"), None),
        P(),
        P(("groups", "docs"), None),
        P(),
        P(),
        P(),
        P(),
        P(),
        P(),
        P(),
        P(),
        P(),
    )
    out_specs = P(("groups", "docs"), ("cent", "sub"), None)
    sizes = tuple(mesh.shape[name] for name in AXES)
    return jax.shard_map(
        functools.partial(on_device, sizes),
        mesh=mesh,
        in_specs=in_specs,
        out_specs=out_specs,
        check_vma=False,
    )
```

```python
import functools

import jax
import jax.numpy as jnp
from jax import lax
from jax.experimental import pallas as pl
from jax.experimental.pallas import tpu as pltpu
from jax.sharding import PartitionSpec as P

DIM = 128
QT = 32
H = 256
HEADS = 4
HEAD = 64
F32 = jnp.float32
BF16 = jnp.bfloat16
NT = (((1,), (1,)), ((), ()))
AXES = ("docs", "cent", "sub")


def iota(shape, axis):
    return lax.broadcasted_iota(jnp.int32, shape, axis)


def column(row):
    n = row.shape[1]
    wide = jnp.broadcast_to(row.astype(F32), (n, n))
    return jnp.sum(jnp.where(iota((n, n), 0) == iota((n, n), 1), wide, 0.0), axis=1, keepdims=True)


def wrap(value, size):
    return value & (size - 1) if size & (size - 1) == 0 else lax.rem(value, size)


def shift(value, size):
    return value >> (size.bit_length() - 1) if size & (size - 1) == 0 else lax.div(value, size)


def lookup(table, index, axis):
    numbers = lax.GatherDimensionNumbers(
        offset_dims=(),
        collapsed_slice_dims=(axis,),
        start_index_map=(axis,),
        operand_batching_dims=(1 - axis,),
        start_indices_batching_dims=(1 - axis,),
    )
    return lax.gather(
        table,
        index[..., None],
        numbers,
        slice_sizes=(1, 1),
        mode=lax.GatherScatterMode.PROMISE_IN_BOUNDS,
    )


def halves(values):
    high = values.astype(BF16)
    return high, (values - high.astype(F32)).astype(BF16)


def mm(a, b):
    return jnp.dot(a, b, preferred_element_type=F32)


def rms(values):
    return lax.rsqrt(jnp.mean(values * values, axis=-1, keepdims=True) + 1e-06)


def kernel(
    sizes,
    queries_hbm,
    codes_hbm,
    ids_hbm,
    counts_hbm,
    centroids,
    buckets_hbm,
    candidates_hbm,
    input_proj_hbm,
    gain_one_hbm,
    query_proj,
    key_proj,
    value_proj,
    output_proj,
    gain_two_hbm,
    up_proj,
    down_proj,
    out,
    queries,
    q_own,
    ids,
    counts,
    buckets,
    candidates,
    input_proj,
    gain_one,
    gain_two,
    codes,
    cent_bf,
    table,
    embed,
    q_all,
    outbox,
    inbox,
    hidden,
    wq,
    wk,
    wv,
    wo,
    wu,
    wd,
    load_sem,
    ids_sem,
    q_sem,
    b_sem,
    far_sem,
):
    n_docs, n_cent, n_sub = sizes
    members = n_cent * n_sub
    total = n_docs * members
    docs_local = codes.shape[0]
    pad = codes.shape[1] * 2 // DIM
    tiles, pairs = docs_local // 8, pad // 2
    rows = docs_local // 4
    cand = candidates.shape[1]
    mine = cand // members

    z = lax.axis_index("docs")
    member = lax.axis_index("cent") * n_sub + lax.axis_index("sub")
    me = z * members + member

    def place(flat):
        return {
            "docs": shift(flat, members),
            "cent": shift(wrap(flat, members), n_sub),
            "sub": wrap(flat, n_sub),
        }

    def each(count, body):
        def step(i, carry):
            body(i)
            return carry

        lax.fori_loop(0, count, step, 0, unroll=count <= 16)

    parts = 4
    cent_rows = centroids.shape[0] // parts
    doc_rows = docs_local // parts
    cent_pieces = [
        (centroids.at[i * cent_rows : (i + 1) * cent_rows], cent_bf.at[i * cent_rows : (i + 1) * cent_rows])
        for i in range(parts)
    ]
    code_pieces = [
        (codes_hbm.at[0, i * doc_rows : (i + 1) * doc_rows], codes.at[i * doc_rows : (i + 1) * doc_rows])
        for i in range(parts)
    ]
    small = [(buckets_hbm, buckets), (counts_hbm, counts), (candidates_hbm, candidates)]
    late = [
        (input_proj_hbm, input_proj),
        (gain_one_hbm, gain_one),
        (gain_two_hbm, gain_two),
        (query_proj, wq),
        (key_proj, wk),
        (value_proj, wv),
        (output_proj, wo),
        (up_proj, wu),
        (down_proj, wd),
    ]
    order = [*small, (queries_hbm, queries), *cent_pieces, *code_pieces, *late]
    first = 4 + 2 * parts
    pulls = [
        pltpu.make_async_copy(src, dst, load_sem.at[i % first]) for i, (src, dst) in enumerate(order)
    ]
    query_pull = pulls[3]
    small_pulls, cent_pulls = pulls[0:3], pulls[4 : 4 + parts]
    code_pulls, late_pulls = pulls[4 + parts : 4 + 2 * parts], pulls[4 + 2 * parts :]
    apart = len(ids)
    for pull in (*small_pulls, *cent_pulls):
        pull.start()
    barrier = pltpu.get_barrier_semaphore()
    lowest = jnp.maximum(z - 1, 0) * members
    greeted = jnp.minimum(z + 2, n_docs) * members - 1

    def greet(i):
        flat = i + jnp.where(i >= me, 1, 0)

        @pl.when(flat >= lowest)
        def _():
            pl.semaphore_signal(barrier, inc=1, device_id=place(flat))

    each(total - 1, greet)

    def tell_below():
        pl.semaphore_signal(far_sem, inc=1, device_id={"docs": z - 1})

    for pull in (code_pulls[0], query_pull):
        pull.start()
    for s in range(apart):
        for t in range(docs_local // apart if apart > 1 else 0):
            pltpu.make_async_copy(
                ids_hbm.at[:, (t * apart + s) * pad : (t * apart + s + 1) * pad],
                ids[s].at[:, t * pad : (t + 1) * pad],
                ids_sem.at[0],
            ).start()
    if apart == 1:
        pltpu.make_async_copy(ids_hbm, ids[0], ids_sem.at[0]).start()
    for pull in code_pulls[1:]:
        pull.start()
    for pull in small_pulls:
        pull.wait()

    live = column(counts[...])
    cand_col = column(candidates[...])
    low_levels, high_levels = buckets[0:8, :], buckets[8:16, :]
    lane = iota((8, DIM), 1)
    words = [(lane >> 1) + 64 * h for h in range(2)]
    nibble = (lane & 1) * 4

    def residual(word, h):
        code = lookup(word, words[h], 1) >> nibble
        level = code & 7
        return jnp.where(
            (code & 8) != 0,
            lookup(high_levels, level, 0),
            lookup(low_levels, level, 0),
        )

    def loop(first, last, body):
        def step(i, carry):
            body(i)
            return carry

        lax.fori_loop(first, last, step, 0)

    block = 256

    def widen(i):
        at = pl.ds(pl.multiple_of(i * block, block), block)
        table[at, :] = cent_bf[at, :].astype(F32)

    for i in range(parts):
        cent_pulls[i].wait()
        loop(i * cent_rows // block, (i + 1) * cent_rows // block, widen)
    sub = iota((8, DIM), 0)

    group = 16 if pairs % 16 == 0 else 2

    steps = pairs // group

    def rebuild(i):
        t, k = shift(i, steps), wrap(i, steps)
        start = t * (8 // apart * pad) + k * (2 * group)
        near_codes = codes.at[
            pl.ds(pl.multiple_of(t * 8, 8), 8),
            pl.ds(pl.multiple_of(k * (group * DIM), group * DIM), group * DIM),
        ]
        near_embed = embed.at[pl.ds(pl.multiple_of(i * (group * 8), group * 8), group * 8)]
        for u in range(0, group, 2):
            at = slice(u * 8, u * 8 + 16)
            both = [[], []]
            for v in range(u, u + 2):
                word = near_codes[:, v * DIM : (v + 1) * DIM]
                for h in range(2):
                    acc = None
                    for s in range(8):
                        slot = ids[s % apart][0, start + (s % (8 // apart) * pad + 2 * v + h)]
                        row = jnp.broadcast_to(table[pl.ds(slot, 1), :], (8, DIM))
                        acc = row if acc is None else jnp.where(sub == s, row, acc)
                    both[h].append(acc + residual(word, h))
            for h in range(2):
                near_embed[at, h * DIM : (h + 1) * DIM] = jnp.concatenate(both[h], axis=0).astype(BF16)

    def q_copy(i):
        to = wrap(member + i + 1, members)
        return pltpu.make_async_remote_copy(
            src_ref=q_own,
            dst_ref=q_all.at[member],
            send_sem=q_sem.at[0],
            recv_sem=q_sem.at[1],
            device_id={"cent": shift(to, n_sub), "sub": wrap(to, n_sub)},
        )

    pltpu.make_async_copy(ids_hbm, ids_hbm, ids_sem.at[0]).wait()
    query_pull.wait()
    q_own[...] = queries[...].astype(BF16)
    for i in range(parts):
        code_pulls[i].wait()
        begin, end = (j * tiles * steps // parts for j in (i, i + 1))
        if i == 0:
            loop(begin, begin + 0, rebuild)
            begin += 0
            pl.semaphore_wait(barrier, greeted)
            each(members - 1, lambda i: q_copy(i).start())
            if n_docs >= 3:
                pl.when(z == n_docs - 2)(tell_below)
        if i == parts - 1 and n_docs >= 4:

            @pl.when((z >= 1) & (z <= n_docs - 3))
            def _():
                pl.semaphore_wait(far_sem, 1)
                tell_below()

        loop(begin, end, rebuild)
        if i == 0:
            for pull in late_pulls:
                pull.start()

    for i in range(2):
        others = q_all.at[0 : members - 1]
        pltpu.make_async_copy(others, others, q_sem.at[i]).wait()
    q_all[member] = q_own[...]
    q_rows = members * QT
    splits = q_rows // DIM
    chunk = min(pairs, 64)
    for n in range(splits):
        q_bf = q_all[n * (DIM // QT) : (n + 1) * (DIM // QT)].reshape(DIM, DIM)
        for t in range(tiles):
            live_t = jnp.broadcast_to(live[t * 8 : t * 8 + 8], (8, DIM))
            bests = [None] * 8
            for k in range(0, pairs, chunk):
                at = (t * pairs + k) * 8
                scores = [
                    lax.dot_general(
                        embed[at : at + chunk * 8, h * DIM : (h + 1) * DIM],
                        q_bf,
                        NT,
                        preferred_element_type=F32,
                    )
                    for h in range(2)
                ]
                for u in range(chunk):
                    for h in range(2):
                        part = scores[h][u * 8 : u * 8 + 8]
                        part = jnp.where(live_t > 2.0 * (k + u) + h, part, -1e30)
                        lane_of = (2 * u + h) % 8
                        old = bests[lane_of]
                        bests[lane_of] = part if old is None else jnp.maximum(old, part)
            while len(bests) > 1:
                bests = [jnp.maximum(a, b) for a, b in zip(bests[::2], bests[1::2])]
            best = bests[0]
            for g in range(4):
                to = t % 4
                moved = best if g == to else pltpu.roll(best, (to - g) * QT % DIM, 1)
                outbox[n * 4 + g, t // 4 * 8 : t // 4 * 8 + 8, to * QT : (to + 1) * QT] = moved[
                    :, to * QT : (to + 1) * QT
                ]

    def b_copy(flat, slot):
        return pltpu.make_async_remote_copy(
            src_ref=outbox.at[shift(flat, members)],
            dst_ref=inbox.at[slot],
            send_sem=b_sem.at[0],
            recv_sem=b_sem.at[1],
            device_id=place(flat),
        )

    def b_start(i):
        b_copy(i + jnp.where(i >= me, 1, 0), me).start()

    near = min(2 * members, total) - 1
    each(near, b_start)
    if n_docs >= 3:

        @pl.when(z == 0)
        def _():
            pl.semaphore_wait(far_sem, 1)

        each(total - 1 - near, lambda i: b_start(near + i))
    inbox[me] = outbox[z]

    docs_all = n_docs * docs_local
    c_int = cand_col.astype(jnp.int32)
    within = c_int % docs_local
    row_of = c_int // docs_local * rows + within // 32 * 8 + within % 8
    lanes_of = within // 8 % 4
    one_hot = (iota((cand, docs_all // 4), 1) == row_of).astype(F32).astype(BF16)
    one_hot = jnp.concatenate([one_hot, one_hot], axis=1)
    for pull in late_pulls:
        pull.wait()
    in_high, in_low = halves(jnp.concatenate([input_proj[...]] * 4, axis=0))
    in_four = jnp.concatenate([in_high, in_high, in_low], axis=0)

    for i in range(2):
        others = inbox.at[0 : total - 1]
        pltpu.make_async_copy(others, others, b_sem.at[i]).wait()
    maxima = jnp.concatenate(
        [
            functools.reduce(jnp.maximum, [inbox[d * members + m] for m in range(members)])
            for d in range(n_docs)
        ],
        axis=0,
    )
    picked = mm(one_hot, jnp.concatenate(halves(maxima), axis=0))
    picked = jnp.where(iota((cand, DIM), 1) // QT == lanes_of, picked, 0.0)
    high, low = halves(picked)
    all_hidden = mm(jnp.concatenate([high, low, high], axis=1), in_four)
    all_scale = rms(all_hidden)
    all_gained = (all_hidden * gain_one[...]).astype(BF16)
    hidden[...] = all_hidden
    here = pl.ds(pl.multiple_of(member * mine, 8), mine)
    hidden_zero = hidden[here, :]
    gained = (hidden_zero * gain_one[...]).astype(BF16)
    k_heads = (mm(all_gained, wk[...]) * all_scale).astype(BF16)
    q_heads = (mm(gained, wq[...]) * rms(hidden_zero)).astype(BF16)
    v_heads = (mm(all_gained, wv[...]) * all_scale).astype(BF16)
    head_of = iota((mine, H), 1) // HEAD
    q_stack = jnp.concatenate(
        [jnp.where(head_of == h, q_heads.astype(F32), 0.0) for h in range(HEADS)], axis=0
    ).astype(BF16)
    att = lax.dot_general(q_stack, k_heads, NT, preferred_element_type=F32) * HEAD ** (-0.5)
    expon = jnp.exp(att - jnp.max(att, axis=-1, keepdims=True))
    mixed = mm(expon.astype(BF16), v_heads) / jnp.sum(expon, axis=-1, keepdims=True)
    attended = functools.reduce(
        jnp.add,
        [
            jnp.where(head_of == h, mixed[h * mine : (h + 1) * mine], 0.0)
            for h in range(HEADS)
        ],
    ).astype(BF16)
    hidden_one = hidden_zero + mm(attended, wo[...])
    gained_two = (hidden_one * gain_two[...]).astype(BF16)
    inner = jax.nn.gelu(mm(gained_two, wu[...]) * rms(hidden_one)).astype(BF16)
    out[0] = hidden_one + mm(inner, wd[...])


def on_device(sizes, *args):
    (queries, codes, ids, counts, centroids, buckets, candidates, input_proj, gain_one) = args[:9]
    (query_proj, key_proj, value_proj, output_proj, gain_two, up_proj, down_proj) = args[9:]
    n_docs, n_cent, n_sub = sizes
    members = n_cent * n_sub
    total = n_docs * members
    docs_local, width = codes.shape[1:]
    cand = candidates.shape[1]
    slots = docs_local * width * 2 // DIM
    apart = 8 if (width * 2 // DIM) % DIM == 0 else 1
    vmem = pl.BlockSpec(memory_space=pltpu.VMEM)
    hbm = pl.BlockSpec(memory_space=pl.ANY)
    weights = (query_proj, key_proj, value_proj, output_proj, up_proj, down_proj)
    return pl.pallas_call(
        functools.partial(kernel, sizes),
        out_shape=pltpu.VMEM((1, cand // members, H), F32),
        in_specs=[hbm] * 16,
        out_specs=vmem,
        scratch_shapes=[
            pltpu.VMEM(queries.shape, F32),
            pltpu.VMEM(queries.shape, BF16),
            [pltpu.SMEM((1, ids.shape[1] // apart), jnp.int32) for _ in range(apart)],
            pltpu.VMEM(counts.shape, jnp.int32),
            pltpu.VMEM(buckets.shape, F32),
            pltpu.VMEM(candidates.shape, jnp.int32),
            pltpu.VMEM(input_proj.shape, F32),
            pltpu.VMEM((1, H), F32),
            pltpu.VMEM((1, H), F32),
            pltpu.VMEM((docs_local, width), jnp.int32),
            pltpu.VMEM(centroids.shape, BF16),
            pltpu.VMEM(centroids.shape, F32),
            pltpu.VMEM((slots // 2, 2 * DIM), BF16),
            pltpu.VMEM((members, QT, DIM), BF16),
            pltpu.VMEM((n_docs, docs_local // 4, DIM), F32),
            pltpu.VMEM((total, docs_local // 4, DIM), F32),
            pltpu.VMEM((cand, H), F32),
            *[pltpu.VMEM(w.shape, BF16) for w in weights],
            pltpu.SemaphoreType.DMA((12,)),
            pltpu.SemaphoreType.DMA((1,)),
            pltpu.SemaphoreType.DMA((2,)),
            pltpu.SemaphoreType.DMA((2,)),
            pltpu.SemaphoreType.REGULAR,
        ],
        compiler_params=pltpu.CompilerParams(collective_id=0, has_side_effects=True),
    )(
        queries,
        codes,
        ids,
        counts,
        centroids,
        buckets,
        candidates,
        input_proj,
        gain_one.reshape(1, H),
        query_proj,
        key_proj,
        value_proj,
        output_proj,
        gain_two.reshape(1, H),
        up_proj,
        down_proj,
    )


def solution(mesh):
    in_specs = (
        P(("groups", "cent", "sub"), None),
        P(("cent", "sub"), ("groups", "docs"), None),
        P(("cent", "sub"), ("groups", "docs")),
        P(("cent", "sub"), ("groups", "docs")),
        P(("cent", "sub"), None),
        P(),
        P(("groups", "docs"), None),
        P(),
        P(),
        P(),
        P(),
        P(),
        P(),
        P(),
        P(),
        P(),
    )
    out_specs = P(("groups", "docs"), ("cent", "sub"), None)
    sizes = tuple(mesh.shape[name] for name in AXES)
    return jax.shard_map(
        functools.partial(on_device, sizes),
        mesh=mesh,
        in_specs=in_specs,
        out_specs=out_specs,
        check_vma=False,
    )
```

```python
import functools

import jax
import jax.numpy as jnp
from jax import lax
from jax.experimental import pallas as pl
from jax.experimental.pallas import tpu as pltpu
from jax.sharding import PartitionSpec as P

DIM = 128
QT = 32
H = 256
HEADS = 4
HEAD = 64
F32 = jnp.float32
BF16 = jnp.bfloat16
NT = (((1,), (1,)), ((), ()))
AXES = ("docs", "cent", "sub")


def iota(shape, axis):
    return lax.broadcasted_iota(jnp.int32, shape, axis)


def column(row):
    n = row.shape[1]
    wide = jnp.broadcast_to(row.astype(F32), (n, n))
    return jnp.sum(jnp.where(iota((n, n), 0) == iota((n, n), 1), wide, 0.0), axis=1, keepdims=True)


def wrap(value, size):
    return value & (size - 1) if size & (size - 1) == 0 else lax.rem(value, size)


def shift(value, size):
    return value >> (size.bit_length() - 1) if size & (size - 1) == 0 else lax.div(value, size)


def lookup(table, index, axis):
    numbers = lax.GatherDimensionNumbers(
        offset_dims=(),
        collapsed_slice_dims=(axis,),
        start_index_map=(axis,),
        operand_batching_dims=(1 - axis,),
        start_indices_batching_dims=(1 - axis,),
    )
    return lax.gather(
        table,
        index[..., None],
        numbers,
        slice_sizes=(1, 1),
        mode=lax.GatherScatterMode.PROMISE_IN_BOUNDS,
    )


def halves(values):
    high = values.astype(BF16)
    return high, (values - high.astype(F32)).astype(BF16)


def mm(a, b):
    return jnp.dot(a, b, preferred_element_type=F32)


def rms(values):
    return lax.rsqrt(jnp.mean(values * values, axis=-1, keepdims=True) + 1e-06)


def kernel(
    sizes,
    queries_hbm,
    codes_hbm,
    ids_hbm,
    counts_hbm,
    centroids,
    buckets_hbm,
    candidates_hbm,
    input_proj_hbm,
    gain_one_hbm,
    query_proj,
    key_proj,
    value_proj,
    output_proj,
    gain_two_hbm,
    up_proj,
    down_proj,
    out,
    queries,
    q_own,
    ids,
    counts,
    buckets,
    candidates,
    input_proj,
    gain_one,
    gain_two,
    codes,
    cent_bf,
    table,
    embed,
    q_all,
    outbox,
    inbox,
    hidden,
    wq,
    wk,
    wv,
    wo,
    wu,
    wd,
    load_sem,
    ids_sem,
    q_sem,
    b_sem,
    far_sem,
):
    n_docs, n_cent, n_sub = sizes
    members = n_cent * n_sub
    total = n_docs * members
    docs_local = codes.shape[0]
    pad = codes.shape[1] * 2 // DIM
    tiles, pairs = docs_local // 8, pad // 2
    rows = docs_local // 4
    cand = candidates.shape[1]
    mine = cand // members

    z = lax.axis_index("docs")
    member = lax.axis_index("cent") * n_sub + lax.axis_index("sub")
    me = z * members + member

    def place(flat):
        return {
            "docs": shift(flat, members),
            "cent": shift(wrap(flat, members), n_sub),
            "sub": wrap(flat, n_sub),
        }

    def each(count, body):
        def step(i, carry):
            body(i)
            return carry

        lax.fori_loop(0, count, step, 0, unroll=count <= 16)

    parts = 4
    cent_parts = 2
    cent_rows = centroids.shape[0] // cent_parts
    doc_rows = docs_local // parts
    cent_pieces = [
        (centroids.at[i * cent_rows : (i + 1) * cent_rows], cent_bf.at[i * cent_rows : (i + 1) * cent_rows])
        for i in range(cent_parts)
    ]
    code_pieces = [
        (codes_hbm.at[0, i * doc_rows : (i + 1) * doc_rows], codes.at[i * doc_rows : (i + 1) * doc_rows])
        for i in range(parts)
    ]
    small = [(buckets_hbm, buckets), (counts_hbm, counts), (candidates_hbm, candidates)]
    late = [
        (input_proj_hbm, input_proj),
        (gain_one_hbm, gain_one),
        (gain_two_hbm, gain_two),
        (query_proj, wq),
        (key_proj, wk),
        (value_proj, wv),
        (output_proj, wo),
        (up_proj, wu),
        (down_proj, wd),
    ]
    order = [*small, (queries_hbm, queries), *cent_pieces, *code_pieces, *late]
    sems = [*range(6 + parts), *range(7), *range(6 + parts, 8 + parts)]
    pulls = [
        pltpu.make_async_copy(src, dst, load_sem.at[sem])
        for sem, (src, dst) in zip(sems, order, strict=True)
    ]
    query_pull = pulls[3]
    small_pulls, cent_pulls = pulls[0:3], pulls[4:6]
    code_pulls, late_pulls = pulls[6 : 6 + parts], pulls[6 + parts :]
    apart = len(ids)
    for pull in (*small_pulls, *cent_pulls):
        pull.start()
    barrier = pltpu.get_barrier_semaphore()
    lowest = jnp.maximum(z - 1, 0) * members
    greeted = jnp.minimum(z + 2, n_docs) * members - 1

    def greet(i):
        flat = i + jnp.where(i >= me, 1, 0)

        @pl.when(flat >= lowest)
        def _():
            pl.semaphore_signal(barrier, inc=1, device_id=place(flat))

    each(total - 1, greet)

    def tell_below():
        pl.semaphore_signal(far_sem, inc=1, device_id={"docs": z - 1})

    for pull in (code_pulls[0], query_pull):
        pull.start()
    for s in range(apart):
        for t in range(docs_local // apart if apart > 1 else 0):
            pltpu.make_async_copy(
                ids_hbm.at[:, (t * apart + s) * pad : (t * apart + s + 1) * pad],
                ids[s].at[:, t * pad : (t + 1) * pad],
                ids_sem.at[0],
            ).start()
    if apart == 1:
        pltpu.make_async_copy(ids_hbm, ids[0], ids_sem.at[0]).start()
    for pull in code_pulls[1:]:
        pull.start()
    for pull in small_pulls:
        pull.wait()

    live = column(counts[...])
    cand_col = column(candidates[...])
    low_levels, high_levels = buckets[0:8, :], buckets[8:16, :]
    lane = iota((8, DIM), 1)
    words = [(lane >> 1) + 64 * h for h in range(2)]
    nibble = (lane & 1) * 4

    def residual(word, h):
        code = lookup(word, words[h], 1) >> nibble
        level = code & 7
        return jnp.where(
            (code & 8) != 0,
            lookup(high_levels, level, 0),
            lookup(low_levels, level, 0),
        )

    def loop(first, last, body):
        def step(i, carry):
            body(i)
            return carry

        lax.fori_loop(first, last, step, 0)

    block = 512

    def widen(i):
        at = pl.ds(pl.multiple_of(i * block, block), block)
        table[at, :] = cent_bf[at, :].astype(F32)

    for i in range(cent_parts):
        cent_pulls[i].wait()
        loop(i * cent_rows // block, (i + 1) * cent_rows // block, widen)
    sub = iota((8, DIM), 0)

    group = 16 if pairs % 16 == 0 else 2

    steps = pairs // group

    def rebuild(i):
        t, k = shift(i, steps), wrap(i, steps)
        start = t * (8 // apart * pad) + k * (2 * group)
        near_codes = codes.at[
            pl.ds(pl.multiple_of(t * 8, 8), 8),
            pl.ds(pl.multiple_of(k * (group * DIM), group * DIM), group * DIM),
        ]
        near_embed = embed.at[pl.ds(pl.multiple_of(i * (group * 8), group * 8), group * 8)]
        for u in range(0, group, 2):
            at = slice(u * 8, u * 8 + 16)
            both = [[], []]
            for v in range(u, u + 2):
                word = near_codes[:, v * DIM : (v + 1) * DIM]
                for h in range(2):
                    acc = None
                    for s in range(8):
                        slot = ids[s % apart][0, start + (s % (8 // apart) * pad + 2 * v + h)]
                        row = jnp.broadcast_to(table[pl.ds(slot, 1), :], (8, DIM))
                        acc = row if acc is None else jnp.where(sub == s, row, acc)
                    both[h].append(acc + residual(word, h))
            for h in range(2):
                near_embed[at, h * DIM : (h + 1) * DIM] = jnp.concatenate(both[h], axis=0).astype(BF16)

    def q_copy(i):
        to = wrap(member + i + 1, members)
        return pltpu.make_async_remote_copy(
            src_ref=q_own,
            dst_ref=q_all.at[member],
            send_sem=q_sem.at[0],
            recv_sem=q_sem.at[1],
            device_id={"cent": shift(to, n_sub), "sub": wrap(to, n_sub)},
        )

    pltpu.make_async_copy(ids_hbm, ids_hbm, ids_sem.at[0]).wait()
    query_pull.wait()
    q_own[...] = queries[...].astype(BF16)
    for i in range(parts):
        code_pulls[i].wait()
        begin, end = (j * tiles * steps // parts for j in (i, i + 1))
        if i == 0:
            loop(begin, begin + 0, rebuild)
            begin += 0
            pl.semaphore_wait(barrier, greeted)
            each(members - 1, lambda i: q_copy(i).start())
            if n_docs >= 3:
                pl.when(z == n_docs - 2)(tell_below)
        if i == parts - 1 and n_docs >= 4:

            @pl.when((z >= 1) & (z <= n_docs - 3))
            def _():
                pl.semaphore_wait(far_sem, 1)
                tell_below()

        middle = end - (end - begin) // 2 if i == parts - 1 else end
        loop(begin, middle, rebuild)
        if i == 0:
            for pull in late_pulls:
                pull.start()

    for i in range(2):
        others = q_all.at[0 : members - 1]
        pltpu.make_async_copy(others, others, q_sem.at[i]).wait()
    q_all[member] = q_own[...]
    q_rows = members * QT
    splits = q_rows // DIM

    def score(n, t):
        q_bf = q_all[n * (DIM // QT) : (n + 1) * (DIM // QT)].reshape(DIM, DIM)
        live_t = jnp.broadcast_to(live[t * 8 : t * 8 + 8], (8, DIM))
        bests = [None] * 8
        at = t * pairs * 8
        scores = [
            lax.dot_general(
                embed[at : at + pairs * 8, h * DIM : (h + 1) * DIM],
                q_bf,
                NT,
                preferred_element_type=F32,
            )
            for h in range(2)
        ]
        for u in range(pairs):
            for h in range(2):
                part = jnp.where(live_t > 2.0 * u + h, scores[h][u * 8 : u * 8 + 8], -1e30)
                lane_of = (2 * u + h) % 8
                old = bests[lane_of]
                bests[lane_of] = part if old is None else jnp.maximum(old, part)
        while len(bests) > 1:
            bests = [jnp.maximum(a, b) for a, b in zip(bests[::2], bests[1::2])]
        best = bests[0]
        for g in range(4):
            to = t % 4
            moved = best if g == to else pltpu.roll(best, (to - g) * QT % DIM, 1)
            outbox[n * 4 + g, t // 4 * 8 : t // 4 * 8 + 8, to * QT : (to + 1) * QT] = moved[
                :, to * QT : (to + 1) * QT
            ]

    done = middle // steps
    for i in range(middle, tiles * steps):
        rebuild(i)
    for n in range(splits):
        for t in range(done):
            score(n, t)
    for n in range(splits):
        for t in range(done, tiles):
            score(n, t)

    def b_copy(flat, slot):
        return pltpu.make_async_remote_copy(
            src_ref=outbox.at[shift(flat, members)],
            dst_ref=inbox.at[slot],
            send_sem=b_sem.at[0],
            recv_sem=b_sem.at[1],
            device_id=place(flat),
        )

    def b_start(i):
        b_copy(i + jnp.where(i >= me, 1, 0), me).start()

    near = min(2 * members, total) - 1
    each(near, b_start)
    if n_docs >= 3:

        @pl.when(z == 0)
        def _():
            pl.semaphore_wait(far_sem, 1)

        each(total - 1 - near, lambda i: b_start(near + i))
    inbox[me] = outbox[z]

    docs_all = n_docs * docs_local
    c_int = cand_col.astype(jnp.int32)
    within = c_int % docs_local
    row_of = c_int // docs_local * rows + within // 32 * 8 + within % 8
    lanes_of = within // 8 % 4
    one_hot = (iota((cand, docs_all // 4), 1) == row_of).astype(F32).astype(BF16)
    one_hot = jnp.concatenate([one_hot, one_hot], axis=1)
    for pull in late_pulls:
        pull.wait()
    in_high, in_low = halves(jnp.concatenate([input_proj[...]] * 4, axis=0))
    in_four = jnp.concatenate([in_high, in_high, in_low], axis=0)

    for i in range(2):
        others = inbox.at[0 : total - 1]
        pltpu.make_async_copy(others, others, b_sem.at[i]).wait()
    maxima = jnp.concatenate(
        [
            functools.reduce(jnp.maximum, [inbox[d * members + m] for m in range(members)])
            for d in range(n_docs)
        ],
        axis=0,
    )
    picked = mm(one_hot, jnp.concatenate(halves(maxima), axis=0))
    picked = jnp.where(iota((cand, DIM), 1) // QT == lanes_of, picked, 0.0)
    high, low = halves(picked)
    all_hidden = mm(jnp.concatenate([high, low, high], axis=1), in_four)
    all_scale = rms(all_hidden)
    all_gained = (all_hidden * gain_one[...]).astype(BF16)
    hidden[...] = all_hidden
    here = pl.ds(pl.multiple_of(member * mine, 8), mine)
    hidden_zero = hidden[here, :]
    gained = (hidden_zero * gain_one[...]).astype(BF16)
    k_heads = (mm(all_gained, wk[...]) * all_scale).astype(BF16)
    q_heads = (mm(gained, wq[...]) * rms(hidden_zero)).astype(BF16)
    v_heads = (mm(all_gained, wv[...]) * all_scale).astype(BF16)
    head_of = iota((mine, H), 1) // HEAD
    q_stack = jnp.concatenate(
        [jnp.where(head_of == h, q_heads.astype(F32), 0.0) for h in range(HEADS)], axis=0
    ).astype(BF16)
    att = lax.dot_general(q_stack, k_heads, NT, preferred_element_type=F32) * HEAD ** (-0.5)
    expon = jnp.exp(att - jnp.max(att, axis=-1, keepdims=True))
    mixed = mm(expon.astype(BF16), v_heads) / jnp.sum(expon, axis=-1, keepdims=True)
    attended = functools.reduce(
        jnp.add,
        [
            jnp.where(head_of == h, mixed[h * mine : (h + 1) * mine], 0.0)
            for h in range(HEADS)
        ],
    ).astype(BF16)
    hidden_one = hidden_zero + mm(attended, wo[...])
    gained_two = (hidden_one * gain_two[...]).astype(BF16)
    inner = jax.nn.gelu(mm(gained_two, wu[...]) * rms(hidden_one)).astype(BF16)
    out[0] = hidden_one + mm(inner, wd[...])


def on_device(sizes, *args):
    (queries, codes, ids, counts, centroids, buckets, candidates, input_proj, gain_one) = args[:9]
    (query_proj, key_proj, value_proj, output_proj, gain_two, up_proj, down_proj) = args[9:]
    n_docs, n_cent, n_sub = sizes
    members = n_cent * n_sub
    total = n_docs * members
    docs_local, width = codes.shape[1:]
    cand = candidates.shape[1]
    slots = docs_local * width * 2 // DIM
    apart = 8 if (width * 2 // DIM) % DIM == 0 else 1
    vmem = pl.BlockSpec(memory_space=pltpu.VMEM)
    hbm = pl.BlockSpec(memory_space=pl.ANY)
    weights = (query_proj, key_proj, value_proj, output_proj, up_proj, down_proj)
    return pl.pallas_call(
        functools.partial(kernel, sizes),
        out_shape=pltpu.VMEM((1, cand // members, H), F32),
        in_specs=[hbm] * 16,
        out_specs=vmem,
        scratch_shapes=[
            pltpu.VMEM(queries.shape, F32),
            pltpu.VMEM(queries.shape, BF16),
            [pltpu.SMEM((1, ids.shape[1] // apart), jnp.int32) for _ in range(apart)],
            pltpu.VMEM(counts.shape, jnp.int32),
            pltpu.VMEM(buckets.shape, F32),
            pltpu.VMEM(candidates.shape, jnp.int32),
            pltpu.VMEM(input_proj.shape, F32),
            pltpu.VMEM((1, H), F32),
            pltpu.VMEM((1, H), F32),
            pltpu.VMEM((docs_local, width), jnp.int32),
            pltpu.VMEM(centroids.shape, BF16),
            pltpu.VMEM(centroids.shape, F32),
            pltpu.VMEM((slots // 2, 2 * DIM), BF16),
            pltpu.VMEM((members, QT, DIM), BF16),
            pltpu.VMEM((n_docs, docs_local // 4, DIM), F32),
            pltpu.VMEM((total, docs_local // 4, DIM), F32),
            pltpu.VMEM((cand, H), F32),
            *[pltpu.VMEM(w.shape, BF16) for w in weights],
            pltpu.SemaphoreType.DMA((12,)),
            pltpu.SemaphoreType.DMA((1,)),
            pltpu.SemaphoreType.DMA((2,)),
            pltpu.SemaphoreType.DMA((2,)),
            pltpu.SemaphoreType.REGULAR,
        ],
        compiler_params=pltpu.CompilerParams(collective_id=0, has_side_effects=True),
    )(
        queries,
        codes,
        ids,
        counts,
        centroids,
        buckets,
        candidates,
        input_proj,
        gain_one.reshape(1, H),
        query_proj,
        key_proj,
        value_proj,
        output_proj,
        gain_two.reshape(1, H),
        up_proj,
        down_proj,
    )


def solution(mesh):
    in_specs = (
        P(("groups", "cent", "sub"), None),
        P(("cent", "sub"), ("groups", "docs"), None),
        P(("cent", "sub"), ("groups", "docs")),
        P(("cent", "sub"), ("groups", "docs")),
        P(("cent", "sub"), None),
        P(),
        P(("groups", "docs"), None),
        P(),
        P(),
        P(),
        P(),
        P(),
        P(),
        P(),
        P(),
        P(),
    )
    out_specs = P(("groups", "docs"), ("cent", "sub"), None)
    sizes = tuple(mesh.shape[name] for name in AXES)
    return jax.shard_map(
        functools.partial(on_device, sizes),
        mesh=mesh,
        in_specs=in_specs,
        out_specs=out_specs,
        check_vma=False,
    )
```

```python
import functools

import jax
import jax.numpy as jnp
from jax import lax
from jax.experimental import pallas as pl
from jax.experimental.pallas import tpu as pltpu
from jax.sharding import PartitionSpec as P

DIM = 128
QT = 32
H = 256
HEADS = 4
HEAD = 64
F32 = jnp.float32
BF16 = jnp.bfloat16
NT = (((1,), (1,)), ((), ()))
AXES = ("docs", "cent", "sub")


def iota(shape, axis):
    return lax.broadcasted_iota(jnp.int32, shape, axis)


def column(row):
    n = row.shape[1]
    wide = jnp.broadcast_to(row.astype(F32), (n, n))
    return jnp.sum(jnp.where(iota((n, n), 0) == iota((n, n), 1), wide, 0.0), axis=1, keepdims=True)


def wrap(value, size):
    return value & (size - 1) if size & (size - 1) == 0 else lax.rem(value, size)


def shift(value, size):
    return value >> (size.bit_length() - 1) if size & (size - 1) == 0 else lax.div(value, size)


def lookup(table, index, axis):
    numbers = lax.GatherDimensionNumbers(
        offset_dims=(),
        collapsed_slice_dims=(axis,),
        start_index_map=(axis,),
        operand_batching_dims=(1 - axis,),
        start_indices_batching_dims=(1 - axis,),
    )
    return lax.gather(
        table,
        index[..., None],
        numbers,
        slice_sizes=(1, 1),
        mode=lax.GatherScatterMode.PROMISE_IN_BOUNDS,
    )


def halves(values):
    high = values.astype(BF16)
    return high, (values - high.astype(F32)).astype(BF16)


def mm(a, b):
    return jnp.dot(a, b, preferred_element_type=F32)


def rms(values):
    return lax.rsqrt(jnp.mean(values * values, axis=-1, keepdims=True) + 1e-06)


def kernel(
    sizes,
    queries_hbm,
    codes_hbm,
    ids_hbm,
    counts_hbm,
    centroids,
    buckets_hbm,
    candidates_hbm,
    input_proj_hbm,
    gain_one_hbm,
    query_proj,
    key_proj,
    value_proj,
    output_proj,
    gain_two_hbm,
    up_proj,
    down_proj,
    out,
    queries,
    q_own,
    ids,
    counts,
    buckets,
    candidates,
    input_proj,
    gain_one,
    gain_two,
    codes,
    cent_bf,
    table,
    embed,
    q_all,
    outbox,
    inbox,
    hidden,
    wq,
    wk,
    wv,
    wo,
    wu,
    wd,
    load_sem,
    ids_sem,
    q_sem,
    b_sem,
    far_sem,
):
    n_docs, n_cent, n_sub = sizes
    members = n_cent * n_sub
    total = n_docs * members
    docs_local = codes.shape[0]
    pad = codes.shape[1] * 2 // DIM
    tiles, pairs = docs_local // 8, pad // 2
    rows = docs_local // 4
    cand = candidates.shape[1]
    mine = cand // members

    z = lax.axis_index("docs")
    member = lax.axis_index("cent") * n_sub + lax.axis_index("sub")
    me = z * members + member

    def place(flat):
        return {
            "docs": shift(flat, members),
            "cent": shift(wrap(flat, members), n_sub),
            "sub": wrap(flat, n_sub),
        }

    def each(count, body):
        def step(i, carry):
            body(i)
            return carry

        lax.fori_loop(0, count, step, 0, unroll=count <= 16)

    parts = 4
    cent_parts = 2
    cent_rows = centroids.shape[0] // cent_parts
    doc_rows = docs_local // parts
    cent_pieces = [
        (centroids.at[i * cent_rows : (i + 1) * cent_rows], cent_bf.at[i * cent_rows : (i + 1) * cent_rows])
        for i in range(cent_parts)
    ]
    code_pieces = [
        (codes_hbm.at[0, i * doc_rows : (i + 1) * doc_rows], codes.at[i * doc_rows : (i + 1) * doc_rows])
        for i in range(parts)
    ]
    small = [(buckets_hbm, buckets), (counts_hbm, counts), (candidates_hbm, candidates)]
    late = [
        (input_proj_hbm, input_proj),
        (gain_one_hbm, gain_one),
        (gain_two_hbm, gain_two),
        (query_proj, wq),
        (key_proj, wk),
        (value_proj, wv),
        (output_proj, wo),
        (up_proj, wu),
        (down_proj, wd),
    ]
    order = [*small, (queries_hbm, queries), *cent_pieces, *code_pieces, *late]
    sems = [*range(6 + parts), *range(7), *range(6 + parts, 8 + parts)]
    pulls = [
        pltpu.make_async_copy(src, dst, load_sem.at[sem])
        for sem, (src, dst) in zip(sems, order, strict=True)
    ]
    query_pull = pulls[3]
    small_pulls, cent_pulls = pulls[0:3], pulls[4:6]
    code_pulls, late_pulls = pulls[6 : 6 + parts], pulls[6 + parts :]
    apart = len(ids)
    for pull in (*small_pulls, *cent_pulls):
        pull.start()
    barrier = pltpu.get_barrier_semaphore()
    lowest = z * members
    greeted = (z + 1) * members - 1

    def greet(i):
        flat = i + jnp.where(i >= me, 1, 0)

        @pl.when(flat >= lowest)
        def _():
            pl.semaphore_signal(barrier, inc=1, device_id=place(flat))

    each(total - 1, greet)

    def tell_below():
        pl.semaphore_signal(far_sem, inc=1, device_id={"docs": z - 1})

    for pull in (code_pulls[0], query_pull):
        pull.start()
    for s in range(apart):
        for t in range(docs_local // apart if apart > 1 else 0):
            pltpu.make_async_copy(
                ids_hbm.at[:, (t * apart + s) * pad : (t * apart + s + 1) * pad],
                ids[s].at[:, t * pad : (t + 1) * pad],
                ids_sem.at[0],
            ).start()
    if apart == 1:
        pltpu.make_async_copy(ids_hbm, ids[0], ids_sem.at[0]).start()
    for pull in code_pulls[1:]:
        pull.start()
    for pull in small_pulls:
        pull.wait()

    live = column(counts[...])
    cand_col = column(candidates[...])
    low_levels, high_levels = buckets[0:8, :], buckets[8:16, :]
    lane = iota((8, DIM), 1)
    words = [(lane >> 1) + 64 * h for h in range(2)]
    nibble = (lane & 1) * 4

    def residual(word, h):
        code = lookup(word, words[h], 1) >> nibble
        level = code & 7
        return jnp.where(
            (code & 8) != 0,
            lookup(high_levels, level, 0),
            lookup(low_levels, level, 0),
        )

    def loop(first, last, body):
        def step(i, carry):
            body(i)
            return carry

        lax.fori_loop(first, last, step, 0)

    block = 512

    def widen(i):
        at = pl.ds(pl.multiple_of(i * block, block), block)
        table[at, :] = cent_bf[at, :].astype(F32)

    def q_copy(i):
        to = wrap(member + i + 1, members)
        return pltpu.make_async_remote_copy(
            src_ref=q_own,
            dst_ref=q_all.at[member],
            send_sem=q_sem.at[0],
            recv_sem=q_sem.at[1],
            device_id={"cent": shift(to, n_sub), "sub": wrap(to, n_sub)},
        )

    for i in range(cent_parts):
        if i == 0:
            query_pull.wait()
            q_own[...] = queries[...].astype(BF16)
            pl.semaphore_wait(barrier, greeted)
            each(members - 1, lambda i: q_copy(i).start())
            if n_docs >= 2:
                pl.when(z == n_docs - 1)(tell_below)
        cent_pulls[i].wait()
        loop(i * cent_rows // block, (i + 1) * cent_rows // block, widen)
    sub = iota((8, DIM), 0)

    group = 16 if pairs % 16 == 0 else 2

    steps = pairs // group

    def rebuild(i):
        t, k = shift(i, steps), wrap(i, steps)
        start = t * (8 // apart * pad) + k * (2 * group)
        near_codes = codes.at[
            pl.ds(pl.multiple_of(t * 8, 8), 8),
            pl.ds(pl.multiple_of(k * (group * DIM), group * DIM), group * DIM),
        ]
        near_embed = embed.at[pl.ds(pl.multiple_of(i * (group * 8), group * 8), group * 8)]
        for u in range(0, group, 2):
            at = slice(u * 8, u * 8 + 16)
            both = [[], []]
            for v in range(u, u + 2):
                word = near_codes[:, v * DIM : (v + 1) * DIM]
                for h in range(2):
                    acc = None
                    for s in range(8):
                        slot = ids[s % apart][0, start + (s % (8 // apart) * pad + 2 * v + h)]
                        row = jnp.broadcast_to(table[pl.ds(slot, 1), :], (8, DIM))
                        acc = row if acc is None else jnp.where(sub == s, row, acc)
                    both[h].append(acc + residual(word, h))
            for h in range(2):
                near_embed[at, h * DIM : (h + 1) * DIM] = jnp.concatenate(both[h], axis=0).astype(BF16)

    pltpu.make_async_copy(ids_hbm, ids_hbm, ids_sem.at[0]).wait()
    for i in range(parts):
        code_pulls[i].wait()
        begin, end = (j * tiles * steps // parts for j in (i, i + 1))
        if i == parts - 1 and n_docs >= 4:

            @pl.when((z >= 2) & (z <= n_docs - 2))
            def _():
                pl.semaphore_wait(far_sem, 1)
                tell_below()

        middle = end - (end - begin) // 2 if i == parts - 1 else end
        loop(begin, middle, rebuild)
        if i == 0:
            for pull in late_pulls:
                pull.start()

    for i in range(2):
        others = q_all.at[0 : members - 1]
        pltpu.make_async_copy(others, others, q_sem.at[i]).wait()
    q_all[member] = q_own[...]
    q_rows = members * QT
    splits = q_rows // DIM

    def score(n, t):
        q_bf = q_all[n * (DIM // QT) : (n + 1) * (DIM // QT)].reshape(DIM, DIM)
        live_t = jnp.broadcast_to(live[t * 8 : t * 8 + 8], (8, DIM))
        bests = [None] * 8
        at = t * pairs * 8
        scores = [
            lax.dot_general(
                embed[at : at + pairs * 8, h * DIM : (h + 1) * DIM],
                q_bf,
                NT,
                preferred_element_type=F32,
            )
            for h in range(2)
        ]
        for u in range(pairs):
            for h in range(2):
                part = jnp.where(live_t > 2.0 * u + h, scores[h][u * 8 : u * 8 + 8], -1e30)
                lane_of = (2 * u + h) % 8
                old = bests[lane_of]
                bests[lane_of] = part if old is None else jnp.maximum(old, part)
        while len(bests) > 1:
            bests = [jnp.maximum(a, b) for a, b in zip(bests[::2], bests[1::2])]
        best = bests[0]
        for g in range(4):
            to = t % 4
            moved = best if g == to else pltpu.roll(best, (to - g) * QT % DIM, 1)
            outbox[n * 4 + g, t // 4 * 8 : t // 4 * 8 + 8, to * QT : (to + 1) * QT] = moved[
                :, to * QT : (to + 1) * QT
            ]

    done = middle // steps
    for i in range(middle, tiles * steps):
        rebuild(i)
    for n in range(splits):
        for t in range(done):
            score(n, t)
    for n in range(splits):
        for t in range(done, tiles):
            score(n, t)

    def b_copy(flat, slot):
        return pltpu.make_async_remote_copy(
            src_ref=outbox.at[shift(flat, members)],
            dst_ref=inbox.at[slot],
            send_sem=b_sem.at[0],
            recv_sem=b_sem.at[1],
            device_id=place(flat),
        )

    def b_start(i):
        b_copy(i + jnp.where(i >= me, 1, 0), me).start()

    if n_docs >= 2:
        bound = [members - 1, min(2 * members, total) - 1, total - 1]
        each(bound[0], b_start)

        @pl.when(z == 0)
        def _():
            pl.semaphore_wait(far_sem, 1)

        each(bound[1] - bound[0], lambda i: b_start(bound[0] + i))
        if n_docs >= 3:

            @pl.when(z == 1)
            def _():
                pl.semaphore_wait(far_sem, 1)
                tell_below()

        each(bound[2] - bound[1], lambda i: b_start(bound[1] + i))
    else:
        each(total - 1, b_start)
    inbox[me] = outbox[z]

    docs_all = n_docs * docs_local
    c_int = cand_col.astype(jnp.int32)
    within = c_int % docs_local
    row_of = c_int // docs_local * rows + within // 32 * 8 + within % 8
    lanes_of = within // 8 % 4
    one_hot = (iota((cand, docs_all // 4), 1) == row_of).astype(F32).astype(BF16)
    one_hot = jnp.concatenate([one_hot, one_hot], axis=1)
    for pull in late_pulls:
        pull.wait()
    in_high, in_low = halves(jnp.concatenate([input_proj[...]] * 4, axis=0))
    in_four = jnp.concatenate([in_high, in_high, in_low], axis=0)

    for i in range(2):
        others = inbox.at[0 : total - 1]
        pltpu.make_async_copy(others, others, b_sem.at[i]).wait()
    maxima = jnp.concatenate(
        [
            functools.reduce(jnp.maximum, [inbox[d * members + m] for m in range(members)])
            for d in range(n_docs)
        ],
        axis=0,
    )
    picked = mm(one_hot, jnp.concatenate(halves(maxima), axis=0))
    picked = jnp.where(iota((cand, DIM), 1) // QT == lanes_of, picked, 0.0)
    high, low = halves(picked)
    all_hidden = mm(jnp.concatenate([high, low, high], axis=1), in_four)
    all_scale = rms(all_hidden)
    all_gained = (all_hidden * gain_one[...]).astype(BF16)
    hidden[...] = all_hidden
    here = pl.ds(pl.multiple_of(member * mine, 8), mine)
    hidden_zero = hidden[here, :]
    gained = (hidden_zero * gain_one[...]).astype(BF16)
    k_heads = (mm(all_gained, wk[...]) * all_scale).astype(BF16)
    q_heads = (mm(gained, wq[...]) * rms(hidden_zero)).astype(BF16)
    v_heads = (mm(all_gained, wv[...]) * all_scale).astype(BF16)
    head_of = iota((mine, H), 1) // HEAD
    q_stack = jnp.concatenate(
        [jnp.where(head_of == h, q_heads.astype(F32), 0.0) for h in range(HEADS)], axis=0
    ).astype(BF16)
    att = lax.dot_general(q_stack, k_heads, NT, preferred_element_type=F32) * HEAD ** (-0.5)
    expon = jnp.exp(att - jnp.max(att, axis=-1, keepdims=True))
    mixed = mm(expon.astype(BF16), v_heads) / jnp.sum(expon, axis=-1, keepdims=True)
    attended = functools.reduce(
        jnp.add,
        [
            jnp.where(head_of == h, mixed[h * mine : (h + 1) * mine], 0.0)
            for h in range(HEADS)
        ],
    ).astype(BF16)
    hidden_one = hidden_zero + mm(attended, wo[...])
    gained_two = (hidden_one * gain_two[...]).astype(BF16)
    inner = jax.nn.gelu(mm(gained_two, wu[...]) * rms(hidden_one)).astype(BF16)
    out[0] = hidden_one + mm(inner, wd[...])


def on_device(sizes, *args):
    (queries, codes, ids, counts, centroids, buckets, candidates, input_proj, gain_one) = args[:9]
    (query_proj, key_proj, value_proj, output_proj, gain_two, up_proj, down_proj) = args[9:]
    n_docs, n_cent, n_sub = sizes
    members = n_cent * n_sub
    total = n_docs * members
    docs_local, width = codes.shape[1:]
    cand = candidates.shape[1]
    slots = docs_local * width * 2 // DIM
    apart = 8 if (width * 2 // DIM) % DIM == 0 else 1
    vmem = pl.BlockSpec(memory_space=pltpu.VMEM)
    hbm = pl.BlockSpec(memory_space=pl.ANY)
    weights = (query_proj, key_proj, value_proj, output_proj, up_proj, down_proj)
    return pl.pallas_call(
        functools.partial(kernel, sizes),
        out_shape=pltpu.VMEM((1, cand // members, H), F32),
        in_specs=[hbm] * 16,
        out_specs=vmem,
        scratch_shapes=[
            pltpu.VMEM(queries.shape, F32),
            pltpu.VMEM(queries.shape, BF16),
            [pltpu.SMEM((1, ids.shape[1] // apart), jnp.int32) for _ in range(apart)],
            pltpu.VMEM(counts.shape, jnp.int32),
            pltpu.VMEM(buckets.shape, F32),
            pltpu.VMEM(candidates.shape, jnp.int32),
            pltpu.VMEM(input_proj.shape, F32),
            pltpu.VMEM((1, H), F32),
            pltpu.VMEM((1, H), F32),
            pltpu.VMEM((docs_local, width), jnp.int32),
            pltpu.VMEM(centroids.shape, BF16),
            pltpu.VMEM(centroids.shape, F32),
            pltpu.VMEM((slots // 2, 2 * DIM), BF16),
            pltpu.VMEM((members, QT, DIM), BF16),
            pltpu.VMEM((n_docs, docs_local // 4, DIM), F32),
            pltpu.VMEM((total, docs_local // 4, DIM), F32),
            pltpu.VMEM((cand, H), F32),
            *[pltpu.VMEM(w.shape, BF16) for w in weights],
            pltpu.SemaphoreType.DMA((12,)),
            pltpu.SemaphoreType.DMA((1,)),
            pltpu.SemaphoreType.DMA((2,)),
            pltpu.SemaphoreType.DMA((2,)),
            pltpu.SemaphoreType.REGULAR,
        ],
        compiler_params=pltpu.CompilerParams(collective_id=0, has_side_effects=True),
    )(
        queries,
        codes,
        ids,
        counts,
        centroids,
        buckets,
        candidates,
        input_proj,
        gain_one.reshape(1, H),
        query_proj,
        key_proj,
        value_proj,
        output_proj,
        gain_two.reshape(1, H),
        up_proj,
        down_proj,
    )


def solution(mesh):
    in_specs = (
        P(("groups", "cent", "sub"), None),
        P(("cent", "sub"), ("groups", "docs"), None),
        P(("cent", "sub"), ("groups", "docs")),
        P(("cent", "sub"), ("groups", "docs")),
        P(("cent", "sub"), None),
        P(),
        P(("groups", "docs"), None),
        P(),
        P(),
        P(),
        P(),
        P(),
        P(),
        P(),
        P(),
        P(),
    )
    out_specs = P(("groups", "docs"), ("cent", "sub"), None)
    sizes = tuple(mesh.shape[name] for name in AXES)
    return jax.shard_map(
        functools.partial(on_device, sizes),
        mesh=mesh,
        in_specs=in_specs,
        out_specs=out_specs,
        check_vma=False,
    )
```

```python
import functools

import jax
import jax.numpy as jnp
from jax import lax
from jax.experimental import pallas as pl
from jax.experimental.pallas import tpu as pltpu
from jax.sharding import PartitionSpec as P

DIM = 128
QT = 32
H = 256
HEADS = 4
HEAD = 64
F32 = jnp.float32
BF16 = jnp.bfloat16
NT = (((1,), (1,)), ((), ()))
AXES = ("docs", "cent", "sub")


def iota(shape, axis):
    return lax.broadcasted_iota(jnp.int32, shape, axis)


def column(row):
    n = row.shape[1]
    wide = jnp.broadcast_to(row.astype(F32), (n, n))
    return jnp.sum(jnp.where(iota((n, n), 0) == iota((n, n), 1), wide, 0.0), axis=1, keepdims=True)


def wrap(value, size):
    return value & (size - 1) if size & (size - 1) == 0 else lax.rem(value, size)


def shift(value, size):
    return value >> (size.bit_length() - 1) if size & (size - 1) == 0 else lax.div(value, size)


def lookup(table, index, axis):
    numbers = lax.GatherDimensionNumbers(
        offset_dims=(),
        collapsed_slice_dims=(axis,),
        start_index_map=(axis,),
        operand_batching_dims=(1 - axis,),
        start_indices_batching_dims=(1 - axis,),
    )
    return lax.gather(
        table,
        index[..., None],
        numbers,
        slice_sizes=(1, 1),
        mode=lax.GatherScatterMode.PROMISE_IN_BOUNDS,
    )


def halves(values):
    high = values.astype(BF16)
    return high, (values - high.astype(F32)).astype(BF16)


def mm(a, b):
    return jnp.dot(a, b, preferred_element_type=F32)


def rms(values):
    return lax.rsqrt(jnp.mean(values * values, axis=-1, keepdims=True) + 1e-06)


def kernel(
    sizes,
    queries_hbm,
    codes_hbm,
    ids_hbm,
    counts_hbm,
    centroids,
    buckets_hbm,
    candidates_hbm,
    input_proj_hbm,
    gain_one_hbm,
    query_proj,
    key_proj,
    value_proj,
    output_proj,
    gain_two_hbm,
    up_proj,
    down_proj,
    out,
    queries,
    q_own,
    ids,
    counts,
    buckets,
    candidates,
    input_proj,
    gain_one,
    gain_two,
    codes,
    cent_bf,
    table,
    embed,
    q_all,
    outbox,
    inbox,
    hidden,
    wq,
    wk,
    wv,
    wo,
    wu,
    wd,
    load_sem,
    ids_sem,
    q_sem,
    b_sem,
    far_sem,
):
    n_docs, n_cent, n_sub = sizes
    members = n_cent * n_sub
    total = n_docs * members
    docs_local = codes.shape[0]
    pad = codes.shape[1] * 2 // DIM
    tiles, pairs = docs_local // 8, pad // 2
    rows = docs_local // 4
    cand = candidates.shape[1]
    mine = cand // members

    z = lax.axis_index("docs")
    member = lax.axis_index("cent") * n_sub + lax.axis_index("sub")
    me = z * members + member

    def place(flat):
        return {
            "docs": shift(flat, members),
            "cent": shift(wrap(flat, members), n_sub),
            "sub": wrap(flat, n_sub),
        }

    def each(count, body):
        def step(i, carry):
            body(i)
            return carry

        lax.fori_loop(0, count, step, 0, unroll=count <= 16)

    parts = 4
    cent_parts = 2
    cent_rows = centroids.shape[0] // cent_parts
    doc_rows = docs_local // parts
    cent_pieces = [
        (centroids.at[i * cent_rows : (i + 1) * cent_rows], cent_bf.at[i * cent_rows : (i + 1) * cent_rows])
        for i in range(cent_parts)
    ]
    code_pieces = [
        (codes_hbm.at[0, i * doc_rows : (i + 1) * doc_rows], codes.at[i * doc_rows : (i + 1) * doc_rows])
        for i in range(parts)
    ]
    small = [(buckets_hbm, buckets), (counts_hbm, counts), (candidates_hbm, candidates)]
    late = [
        (input_proj_hbm, input_proj),
        (gain_one_hbm, gain_one),
        (gain_two_hbm, gain_two),
        (query_proj, wq),
        (key_proj, wk),
        (value_proj, wv),
        (output_proj, wo),
        (up_proj, wu),
        (down_proj, wd),
    ]
    order = [*small, (queries_hbm, queries), *cent_pieces, *code_pieces, *late]
    sems = [*range(6 + parts), *range(7), *range(6 + parts, 8 + parts)]
    pulls = [
        pltpu.make_async_copy(src, dst, load_sem.at[sem])
        for sem, (src, dst) in zip(sems, order, strict=True)
    ]
    query_pull = pulls[3]
    small_pulls, cent_pulls = pulls[0:3], pulls[4:6]
    code_pulls, late_pulls = pulls[6 : 6 + parts], pulls[6 + parts :]
    apart = len(ids)
    for pull in (*small_pulls, *cent_pulls):
        pull.start()
    barrier = pltpu.get_barrier_semaphore()
    lowest = z * members
    greeted = (z + 1) * members - 1

    def greet(i):
        flat = i + jnp.where(i >= me, 1, 0)

        @pl.when(flat >= lowest)
        def _():
            pl.semaphore_signal(barrier, inc=1, device_id=place(flat))

    each(total - 1, greet)

    def tell_below():
        pl.semaphore_signal(far_sem, inc=1, device_id={"docs": z - 1})

    for pull in (code_pulls[0], query_pull):
        pull.start()
    for s in range(apart):
        for t in range(docs_local // apart if apart > 1 else 0):
            pltpu.make_async_copy(
                ids_hbm.at[:, (t * apart + s) * pad : (t * apart + s + 1) * pad],
                ids[s].at[:, t * pad : (t + 1) * pad],
                ids_sem.at[0],
            ).start()
    if apart == 1:
        pltpu.make_async_copy(ids_hbm, ids[0], ids_sem.at[0]).start()
    for pull in code_pulls[1:]:
        pull.start()
    for pull in small_pulls:
        pull.wait()

    live = column(counts[...])
    cand_col = column(candidates[...])
    low_levels, high_levels = buckets[0:8, :], buckets[8:16, :]
    lane = iota((8, DIM), 1)
    words = [(lane >> 1) + 64 * h for h in range(2)]
    nibble = (lane & 1) * 4

    def residual(word, h):
        code = lookup(word, words[h], 1) >> nibble
        level = code & 7
        return jnp.where(
            (code & 8) != 0,
            lookup(high_levels, level, 0),
            lookup(low_levels, level, 0),
        )

    def loop(first, last, body):
        def step(i, carry):
            body(i)
            return carry

        lax.fori_loop(first, last, step, 0)

    block = 512

    def widen(i):
        at = pl.ds(pl.multiple_of(i * block, block), block)
        table[at, :] = cent_bf[at, :].astype(F32)

    def q_copy(i):
        to = wrap(member + i + 1, members)
        return pltpu.make_async_remote_copy(
            src_ref=q_own,
            dst_ref=q_all.at[member],
            send_sem=q_sem.at[0],
            recv_sem=q_sem.at[1],
            device_id={"cent": shift(to, n_sub), "sub": wrap(to, n_sub)},
        )

    for i in range(cent_parts):
        if i == 0:
            query_pull.wait()
            q_own[...] = queries[...].astype(BF16)
            pl.semaphore_wait(barrier, greeted)
            each(members - 1, lambda i: q_copy(i).start())
            if n_docs >= 2:
                pl.when(z == n_docs - 1)(tell_below)
        cent_pulls[i].wait()
        loop(i * cent_rows // block, (i + 1) * cent_rows // block, widen)
    sub = iota((8, DIM), 0)

    group = next(g for g in (32, 16, 2) if pairs % g == 0)

    steps = pairs // group

    def rebuild(i):
        t, k = shift(i, steps), wrap(i, steps)
        start = t * (8 // apart * pad) + k * (2 * group)
        near_codes = codes.at[
            pl.ds(pl.multiple_of(t * 8, 8), 8),
            pl.ds(pl.multiple_of(k * (group * DIM), group * DIM), group * DIM),
        ]
        near_embed = embed.at[pl.ds(pl.multiple_of(i * (group * 8), group * 8), group * 8)]
        for u in range(0, group, 2):
            at = slice(u * 8, u * 8 + 16)
            both = [[], []]
            for v in range(u, u + 2):
                word = near_codes[:, v * DIM : (v + 1) * DIM]
                for h in range(2):
                    acc = None
                    for s in range(8):
                        slot = ids[s % apart][0, start + (s % (8 // apart) * pad + 2 * v + h)]
                        row = jnp.broadcast_to(table[pl.ds(slot, 1), :], (8, DIM))
                        acc = row if acc is None else jnp.where(sub == s, row, acc)
                    both[h].append(acc + residual(word, h))
            for h in range(2):
                near_embed[at, h * DIM : (h + 1) * DIM] = jnp.concatenate(both[h], axis=0).astype(BF16)

    pltpu.make_async_copy(ids_hbm, ids_hbm, ids_sem.at[0]).wait()
    for i in range(parts):
        code_pulls[i].wait()
        begin, end = (j * tiles * steps // parts for j in (i, i + 1))
        if i == parts - 1 and n_docs >= 4:

            @pl.when((z >= 2) & (z <= n_docs - 2))
            def _():
                pl.semaphore_wait(far_sem, 1)
                tell_below()

        middle = end - (end - begin) // 2 if i == parts - 1 else end
        loop(begin, middle, rebuild)
        if i == 0:
            for pull in late_pulls:
                pull.start()

    for i in range(2):
        others = q_all.at[0 : members - 1]
        pltpu.make_async_copy(others, others, q_sem.at[i]).wait()
    q_all[member] = q_own[...]
    q_rows = members * QT
    splits = q_rows // DIM

    def score(n, t):
        q_bf = q_all[n * (DIM // QT) : (n + 1) * (DIM // QT)].reshape(DIM, DIM)
        live_t = jnp.broadcast_to(live[t * 8 : t * 8 + 8], (8, DIM))
        bests = [None] * 8
        at = t * pairs * 8
        scores = [
            lax.dot_general(
                embed[at : at + pairs * 8, h * DIM : (h + 1) * DIM],
                q_bf,
                NT,
                preferred_element_type=F32,
            )
            for h in range(2)
        ]
        for u in range(pairs):
            for h in range(2):
                part = jnp.where(live_t > 2.0 * u + h, scores[h][u * 8 : u * 8 + 8], -1e30)
                lane_of = (2 * u + h) % 8
                old = bests[lane_of]
                bests[lane_of] = part if old is None else jnp.maximum(old, part)
        while len(bests) > 1:
            bests = [jnp.maximum(a, b) for a, b in zip(bests[::2], bests[1::2])]
        best = bests[0]
        for g in range(4):
            to = t % 4
            moved = best if g == to else pltpu.roll(best, (to - g) * QT % DIM, 1)
            outbox[n * 4 + g, t // 4 * 8 : t // 4 * 8 + 8, to * QT : (to + 1) * QT] = moved[
                :, to * QT : (to + 1) * QT
            ]

    done = middle // steps
    for i in range(middle, tiles * steps):
        rebuild(i)
    for n in range(splits):
        for t in range(done):
            score(n, t)
    for n in range(splits):
        for t in range(done, tiles):
            score(n, t)

    def b_copy(flat, slot):
        return pltpu.make_async_remote_copy(
            src_ref=outbox.at[shift(flat, members)],
            dst_ref=inbox.at[slot],
            send_sem=b_sem.at[0],
            recv_sem=b_sem.at[1],
            device_id=place(flat),
        )

    def b_start(i):
        b_copy(i + jnp.where(i >= me, 1, 0), me).start()

    if n_docs >= 2:
        bound = [members - 1, min(2 * members, total) - 1, total - 1]
        each(bound[0], b_start)

        @pl.when(z == 0)
        def _():
            pl.semaphore_wait(far_sem, 1)

        each(bound[1] - bound[0], lambda i: b_start(bound[0] + i))
        if n_docs >= 3:

            @pl.when(z == 1)
            def _():
                pl.semaphore_wait(far_sem, 1)
                tell_below()

        each(bound[2] - bound[1], lambda i: b_start(bound[1] + i))
    else:
        each(total - 1, b_start)
    inbox[me] = outbox[z]

    docs_all = n_docs * docs_local
    c_int = cand_col.astype(jnp.int32)
    within = c_int % docs_local
    row_of = c_int // docs_local * rows + within // 32 * 8 + within % 8
    lanes_of = within // 8 % 4
    one_hot = (iota((cand, docs_all // 4), 1) == row_of).astype(F32).astype(BF16)
    one_hot = jnp.concatenate([one_hot, one_hot], axis=1)
    for pull in late_pulls:
        pull.wait()
    in_high, in_low = halves(jnp.concatenate([input_proj[...]] * 4, axis=0))
    in_four = jnp.concatenate([in_high, in_high, in_low], axis=0)

    for i in range(2):
        others = inbox.at[0 : total - 1]
        pltpu.make_async_copy(others, others, b_sem.at[i]).wait()
    maxima = jnp.concatenate(
        [
            functools.reduce(jnp.maximum, [inbox[d * members + m] for m in range(members)])
            for d in range(n_docs)
        ],
        axis=0,
    )
    picked = mm(one_hot, jnp.concatenate(halves(maxima), axis=0))
    picked = jnp.where(iota((cand, DIM), 1) // QT == lanes_of, picked, 0.0)
    high, low = halves(picked)
    all_hidden = mm(jnp.concatenate([high, low, high], axis=1), in_four)
    all_scale = rms(all_hidden)
    all_gained = (all_hidden * gain_one[...]).astype(BF16)
    hidden[...] = all_hidden
    here = pl.ds(pl.multiple_of(member * mine, 8), mine)
    hidden_zero = hidden[here, :]
    gained = (hidden_zero * gain_one[...]).astype(BF16)
    k_heads = (mm(all_gained, wk[...]) * all_scale).astype(BF16)
    q_heads = (mm(gained, wq[...]) * rms(hidden_zero)).astype(BF16)
    v_heads = mm(all_gained, wv[...]) * all_scale
    head_of = iota((mine, H), 1) // HEAD
    v_head_of = iota((cand, H), 1) // HEAD
    v_stack = jnp.concatenate(
        [jnp.where(v_head_of == h, v_heads, 0.0) for h in range(HEADS)], axis=0
    ).astype(BF16)
    v_out = mm(v_stack, wo[...]).astype(BF16)
    q_stack = jnp.concatenate(
        [jnp.where(head_of == h, q_heads.astype(F32), 0.0) for h in range(HEADS)], axis=0
    ).astype(BF16)
    att = lax.dot_general(q_stack, k_heads, NT, preferred_element_type=F32) * HEAD ** (-0.5)
    expon = jnp.exp(att - jnp.max(att, axis=-1, keepdims=True))
    summed = jnp.sum(expon, axis=-1, keepdims=True)
    weights = expon.astype(BF16)
    hidden_one = hidden_zero + functools.reduce(
        jnp.add,
        [
            mm(weights[h * mine : (h + 1) * mine], v_out[h * cand : (h + 1) * cand])
            / summed[h * mine : (h + 1) * mine]
            for h in range(HEADS)
        ],
    )
    gained_two = (hidden_one * gain_two[...]).astype(BF16)
    inner = jax.nn.gelu(mm(gained_two, wu[...]) * rms(hidden_one)).astype(BF16)
    out[0] = hidden_one + mm(inner, wd[...])


def on_device(sizes, *args):
    (queries, codes, ids, counts, centroids, buckets, candidates, input_proj, gain_one) = args[:9]
    (query_proj, key_proj, value_proj, output_proj, gain_two, up_proj, down_proj) = args[9:]
    n_docs, n_cent, n_sub = sizes
    members = n_cent * n_sub
    total = n_docs * members
    docs_local, width = codes.shape[1:]
    cand = candidates.shape[1]
    slots = docs_local * width * 2 // DIM
    apart = 8 if (width * 2 // DIM) % DIM == 0 else 1
    vmem = pl.BlockSpec(memory_space=pltpu.VMEM)
    hbm = pl.BlockSpec(memory_space=pl.ANY)
    weights = (query_proj, key_proj, value_proj, output_proj, up_proj, down_proj)
    return pl.pallas_call(
        functools.partial(kernel, sizes),
        out_shape=pltpu.VMEM((1, cand // members, H), F32),
        in_specs=[hbm] * 16,
        out_specs=vmem,
        scratch_shapes=[
            pltpu.VMEM(queries.shape, F32),
            pltpu.VMEM(queries.shape, BF16),
            [pltpu.SMEM((1, ids.shape[1] // apart), jnp.int32) for _ in range(apart)],
            pltpu.VMEM(counts.shape, jnp.int32),
            pltpu.VMEM(buckets.shape, F32),
            pltpu.VMEM(candidates.shape, jnp.int32),
            pltpu.VMEM(input_proj.shape, F32),
            pltpu.VMEM((1, H), F32),
            pltpu.VMEM((1, H), F32),
            pltpu.VMEM((docs_local, width), jnp.int32),
            pltpu.VMEM(centroids.shape, BF16),
            pltpu.VMEM(centroids.shape, F32),
            pltpu.VMEM((slots // 2, 2 * DIM), BF16),
            pltpu.VMEM((members, QT, DIM), BF16),
            pltpu.VMEM((n_docs, docs_local // 4, DIM), F32),
            pltpu.VMEM((total, docs_local // 4, DIM), F32),
            pltpu.VMEM((cand, H), F32),
            *[pltpu.VMEM(w.shape, BF16) for w in weights],
            pltpu.SemaphoreType.DMA((12,)),
            pltpu.SemaphoreType.DMA((1,)),
            pltpu.SemaphoreType.DMA((2,)),
            pltpu.SemaphoreType.DMA((2,)),
            pltpu.SemaphoreType.REGULAR,
        ],
        compiler_params=pltpu.CompilerParams(collective_id=0, has_side_effects=True),
    )(
        queries,
        codes,
        ids,
        counts,
        centroids,
        buckets,
        candidates,
        input_proj,
        gain_one.reshape(1, H),
        query_proj,
        key_proj,
        value_proj,
        output_proj,
        gain_two.reshape(1, H),
        up_proj,
        down_proj,
    )


def solution(mesh):
    in_specs = (
        P(("groups", "cent", "sub"), None),
        P(("cent", "sub"), ("groups", "docs"), None),
        P(("cent", "sub"), ("groups", "docs")),
        P(("cent", "sub"), ("groups", "docs")),
        P(("cent", "sub"), None),
        P(),
        P(("groups", "docs"), None),
        P(),
        P(),
        P(),
        P(),
        P(),
        P(),
        P(),
        P(),
        P(),
    )
    out_specs = P(("groups", "docs"), ("cent", "sub"), None)
    sizes = tuple(mesh.shape[name] for name in AXES)
    return jax.shard_map(
        functools.partial(on_device, sizes),
        mesh=mesh,
        in_specs=in_specs,
        out_specs=out_specs,
        check_vma=False,
    )
```
